512 devices in a mesh: grp: 32 (over x_hi, y, core), die: 16 (over x_lo, z).
Axes of the slice: x: 4 (x_hi: 2, x_lo: 2; x = x_hi * 2 + x_lo), y: 8, z: 8, core: 2. Of those that a mesh axis runs over, the one named last changes fastest.
Arguments:
- die_volt: float32 [4096, 4096], P('grp', 'die'), may hold values from -6 to 6
- die_load: float32 [4096, 4096], P('grp', 'die'), may hold values from 0.05 to 1
- die_shunt: float32 [4096, 4096], P('grp', 'die'), may hold values from 0.1 to 1
- bump_node: int32 [32768, 128], P(('grp', 'die')), may hold values from -1 to 32767, as said below
- bump_block: int32 [32768], P(('grp', 'die')), may hold values from 0 to 16383, as said below
- bump_cond: float32 [32768, 128], P(('grp', 'die')), may hold values from 0.3 to 3
- pkg_volt: float32 [16384, 128], P('die'), may hold values from -6 to 6
- pkg_diag: float32 [16384, 128], P('die'), may hold values from 4 to 6
- pkg_pattern: int32 [4, 16384], P(None, 'die'), may hold values from 0 to 16383, as said below
- pkg_weight: float32 [4, 16384], P(None, 'die'), may hold values from -0.5 to 0.5
- block_coupling: float32 [128, 128], replicated, may hold values from -0.5 to 0.5
Outputs:
- die_out: float32 [4096, 4096], P('grp', 'die')
- pkg_out: float32 [16384, 128], P('die')
- bump_out: float32 [32768, 128], P(('grp', 'die'))
The draws below stay inside these ranges and needn't reach their ends.
Inputs may be any that keep to these rules, and one draw needn't show every extreme that they name: `bump_node`: live slots of a block come first; each block has 52 or more live slots. `bump_block`: bump block j of a device (j counted within the device) targets a package block of die shard j // 4, that is a block b with b // 1024 = j // 4. pkg_pattern[k, b] lies within 32 blocks of b.
All inputs are finite; a program needn't handle non-finite values.
Results may differ from the reference program's by a relative error of at most 0.0001.
Values sent between devices are 32-bit elements; how exact they have to be, the bound alone decides.
A program may use at most 64 MiB of HBM per device.

```python
import math
import jax
import jax.numpy as jnp
from jax import lax

CX = 128
CY = 256
BUMPBLK = 64
KNB = 4
RADIUS = 32
SWEEPS = 4
ITERS = 4
NX = 4096
NY = 4096
CELLS = 32768
SLOTBLK = 32768
CAP = 4
PB = 16384
PBD = 1024
N_DIE = 16


def draw_bump_node(key, part):
    key_node, key_count = jax.random.split(jax.random.fold_in(key, 11))
    chosen = jax.random.randint(key_node, (SLOTBLK, 128), 0, CELLS, dtype=jnp.int32)
    counted = jax.random.randint(key_count, (SLOTBLK, 1), 52, 129, dtype=jnp.int32)
    lanes = jnp.arange(128, dtype=jnp.int32)[None, :]
    chosen = jnp.where(lanes < counted, chosen, -1)
    chosen = chosen.at[0, 0].set(CELLS - 1)
    chosen = chosen.at[0, 127].set(-1)
    return chosen


def draw_bump_block(key, part):
    offsets = jax.random.randint(jax.random.fold_in(key, 23), (SLOTBLK,), 0, PBD, dtype=jnp.int32)
    within = jnp.arange(SLOTBLK, dtype=jnp.int32) % BUMPBLK
    owner = within // CAP
    blocks = owner * PBD + offsets
    blocks = blocks.at[0].set(0)
    blocks = blocks.at[BUMPBLK - 1].set(PB - 1)
    return blocks


def draw_pkg_pattern(key, part):
    offsets = jax.random.randint(jax.random.fold_in(key, 37), (KNB, PB), -RADIUS, RADIUS + 1, dtype=jnp.int32)
    blocks = jnp.arange(PB, dtype=jnp.int32)
    reach = jnp.where(blocks % 2 == 0, -RADIUS, RADIUS).astype(jnp.int32)
    offsets = offsets.at[0].set(reach)
    return jnp.clip(blocks[None, :] + offsets, 0, PB - 1).astype(jnp.int32)


def levels(key, extent, shards, smallest, top_value):
    factor_of, own = 1.0, jax.random.fold_in(key, 6)
    for axis_at, shards_of in shards:
        draws = jnp.exp(jax.random.uniform(jax.random.fold_in(own, axis_at), (shards_of,), jnp.float32, smallest / len(shards), top_value / len(shards)))
        factor_of = factor_of * jnp.repeat(draws, extent[axis_at] // shards_of).reshape([-1 if axis == axis_at else 1 for axis in range(len(extent))])
    return factor_of


def normal_values(rng, shape, deviation, bound, cuts=(), held_as=jnp.bfloat16):
    entries = deviation * jax.random.normal(rng, shape, jnp.float32)
    if cuts:
        entries = entries * levels(rng, shape, cuts, -0.22, 0.18)
    return jnp.clip(entries, -bound, bound).astype(held_as)


def setup_inputs(seed: int = 0) -> dict:
    arg_keys = jax.random.split(jax.random.key(seed), 12)
    die_volt = normal_values(arg_keys[0], (NX, NY), 1.0, 6.0, ((0, 32), (1, 16)), jnp.float32)
    die_load = jnp.clip(jnp.exp(math.log(1.0) - 2.9957323 * jax.random.uniform(arg_keys[1], (NX, NY), jnp.float32) ** levels(arg_keys[1], (NX, NY), ((0, 32), (1, 16)), -0.2, 0.2)), 0.05, 1.0)
    die_shunt = jnp.clip(jnp.exp(math.log(1.0) - 2.3025851 * jax.random.uniform(arg_keys[2], (NX, NY), jnp.float32) ** levels(arg_keys[2], (NX, NY), ((0, 32), (1, 16)), -0.2, 0.2)), 0.1, 1.0)
    bump_node = draw_bump_node(jax.random.fold_in(arg_keys[11], 71), 0)
    bump_block = draw_bump_block(jax.random.fold_in(arg_keys[11], 71), 0)
    bump_cond = jnp.clip(jnp.exp(math.log(3.0) - 2.3025851 * jax.random.uniform(arg_keys[5], (SLOTBLK, 128), jnp.float32) ** levels(arg_keys[5], (SLOTBLK, 128), ((0, 512),), -0.2, 0.2)), 0.3, 3.0)
    pkg_volt = normal_values(arg_keys[6], (PB, 128), 1.0, 6.0, ((0, 16),), jnp.float32)
    pkg_diag = jnp.clip(4.0 + 2.0 * jax.random.uniform(arg_keys[7], (PB, 128), jnp.float32) ** levels(arg_keys[7], (PB, 128), ((0, 16),), -0.2, 0.2), 4.0, 6.0)
    pkg_pattern = draw_pkg_pattern(jax.random.fold_in(arg_keys[11], 71), 0)
    pkg_weight = jnp.clip(jax.random.uniform(arg_keys[9], (KNB, PB), jnp.float32, -0.5, 0.5) * levels(arg_keys[9], (KNB, PB), ((1, 16),), -0.4, 0.0), -0.5, 0.5)
    block_coupling = normal_values(arg_keys[10], (128, 128), 128 ** -0.5, 0.5, (), jnp.float32)
    return {"die_volt": die_volt, "die_load": die_load, "die_shunt": die_shunt, "bump_node": bump_node, "bump_block": bump_block, "bump_cond": bump_cond, "pkg_volt": pkg_volt, "pkg_diag": pkg_diag, "pkg_pattern": pkg_pattern, "pkg_weight": pkg_weight, "block_coupling": block_coupling}


def sweep_weights(sweeps):
    return [1.0 / (1.0 + 0.8 * math.cos(math.pi * (2 * index + 1) / (2 * sweeps))) for index in range(sweeps)]


def reference(die_volt, die_load, die_shunt, bump_node, bump_block, bump_cond, pkg_volt, pkg_diag, pkg_pattern, pkg_weight, block_coupling):
    live_slot = bump_node >= 0
    safe_node = jnp.where(live_slot, bump_node, 0).astype(jnp.int32)
    device = (jnp.arange(SLOTBLK, dtype=jnp.int32) // BUMPBLK)[:, None]
    row_index = (device // N_DIE) * CX + safe_node // CY
    col_index = (device % N_DIE) * CY + safe_node % CY
    conductance = jnp.where(live_slot, bump_cond, jnp.float32(0.0))
    bump_start = pkg_volt[bump_block]
    grid_zero = jnp.zeros((NX, NY), jnp.float32)
    gsum = grid_zero.at[row_index, col_index].add(conductance)
    inject = grid_zero.at[row_index, col_index].add(conductance * bump_start)
    diagonal = 4.0 + die_shunt + gsum
    right_side = inject - die_load
    voltage = die_volt
    for weight in sweep_weights(SWEEPS):
        padded = jnp.pad(voltage, 1)
        beside = padded[2:, 1:-1] + padded[:-2, 1:-1] + padded[1:-1, 2:] + padded[1:-1, :-2]
        voltage = voltage + weight * (right_side - diagonal * voltage + beside) / diagonal
    at_bump = voltage[row_index, col_index]
    current = conductance * (bump_start - at_bump)
    inflow = jnp.zeros((PB, 128), jnp.float32).at[bump_block].add(current)
    plane = pkg_volt
    for iteration in range(ITERS):
        coupled = jnp.dot(plane, block_coupling, precision=lax.Precision.HIGHEST, preferred_element_type=jnp.float32)
        for neighbour in range(KNB):
            coupled = coupled + pkg_weight[neighbour][:, None] * plane[pkg_pattern[neighbour]]
        plane = (-inflow - coupled) / pkg_diag
    bump_out = plane[bump_block]
    return voltage, plane, bump_out
```

```python
import functools
import math

import jax
import jax.numpy as jnp
from jax import lax
from jax.experimental import pallas as pl
from jax.experimental.pallas import tpu as pltpu
from jax.sharding import PartitionSpec as P

SWEEPS = 4
ITERS = 4
MESH = pl.DeviceIdType.MESH
F32 = jnp.float32
BF16 = jnp.bfloat16


def sweep_weights(sweeps):
    return [
        1.0 / (1.0 + 0.8 * math.cos(math.pi * (2 * index + 1) / (2 * sweeps)))
        for index in range(sweeps)
    ]


def split(x):
    hi = x.astype(BF16)
    lo = (x - hi.astype(F32)).astype(BF16)
    return hi, lo


def remote(src, dst, send_sem, recv_sem, **device):
    return pltpu.make_async_remote_copy(
        src_ref=src,
        dst_ref=dst,
        send_sem=send_sem,
        recv_sem=recv_sem,
        device_id=device,
        device_id_type=MESH,
    )


def signal(barrier, **device):
    pl.semaphore_signal(barrier, inc=1, device_id=device, device_id_type=MESH)


def pick_rows(ids, first, planes, into):
    lane = lax.broadcasted_iota(jnp.int32, ids.shape, 1) + first
    into[...] = jnp.zeros_like(into)

    def step(c, carry):
        start = pl.multiple_of(c * 256, 256)
        onehot = jnp.concatenate(
            [
                jnp.where(ids == lane + (start + part), 1.0, 0.0).astype(BF16)
                for part in (0, 128)
            ],
            axis=1,
        )
        both = jnp.dot(onehot, planes[pl.ds(start, 256), :], preferred_element_type=F32)
        into[...] += both[:, :128] + both[:, 128:]
        return carry

    lax.fori_loop(0, planes.shape[0] // 256, step, 0)


class Exchange:
    def __init__(self, count, me, src, dst, send_sem, recv_sem):
        self.count, self.me = count, me
        self.src, self.dst = src, dst
        self.send_sem, self.recv_sem = send_sem, recv_sem

    def copy(self, k):
        to = lax.rem(self.me + k, self.count)
        return remote(
            self.src.at[to],
            self.dst.at[self.me],
            self.send_sem.at[k],
            self.recv_sem.at[k],
            die=to,
        )

    def start(self):
        for k in range(1, self.count):
            self.copy(k).start()
        self.dst[self.me] = self.src[self.me]

    def wait(self):
        for k in range(1, self.count):
            self.copy(k).wait_recv()

    def drain(self):
        for k in range(1, self.count):
            self.copy(k).wait_send()


def die_kernel(
    nd, ng, cap, blocks,
    volt_ref, load_ref, shunt_ref, node_ref, ids_ref, cond_ref, pkg_ref,
    out_ref, item_ref, rids_ref,
    ids_got, rows_out, rows_got, cur_out, cur_got,
    start_ref, planes, onecol, acc, vx, rx, dx, edge_n, edge_s, edge_w, edge_e,
    halo_n, halo_s, halo_w, halo_e, halo_nw, halo_ne, halo_sw, halo_se,
    sem_ids, sem_rows, sem_cur, sem_halo,
):
    me, mg = lax.axis_index("die"), lax.axis_index("grp")
    rows, cols = volt_ref.shape
    nblk = node_ref.shape[0]
    up, down = lax.rem(mg + ng - 1, ng), lax.rem(mg + 1, ng)
    west, east = lax.rem(me + nd - 1, nd), lax.rem(me + 1, nd)
    barrier = pltpu.get_barrier_semaphore()
    for k in range(1, nd):
        signal(barrier, die=lax.rem(me + k, nd))
    for g in (up, down):
        for d in (west, me, east):
            signal(barrier, grp=g, die=d)

    chunk = 8
    steps = nblk // chunk

    def one_columns(it, carry):
        node = node_ref[pl.ds(pl.multiple_of(it * chunk, chunk), chunk), :]
        col = jnp.bitwise_and(node, cols - 1)
        for i in range(chunk):
            iota = lax.broadcasted_iota(jnp.int32, (cols, 128), 0)
            onecol[it * chunk + i] = jnp.where(iota == col[i : i + 1, :], 1.0, 0.0).astype(BF16)
        return carry

    lax.fori_loop(0, steps, one_columns, 0)
    pl.semaphore_wait(barrier, nd - 1 + 6)

    ids = Exchange(nd, me, ids_ref, ids_got, sem_ids.at[0], sem_ids.at[1])
    ids.start()

    row_iota = lax.broadcasted_iota(jnp.int32, (rows, 128), 0)

    def scatter(value_of, slot):
        def step(it, carry):
            at = pl.ds(pl.multiple_of(it * chunk, chunk), chunk)
            node = node_ref[at, :]
            row = jnp.right_shift(node, cols.bit_length() - 1)
            hi, lo = [v.astype(F32) for v in split(value_of(at))]
            parts_hi, parts_lo = [], []
            for i in range(chunk):
                here = row_iota == row[i : i + 1, :]
                parts_hi.append(jnp.where(here, hi[i : i + 1, :], 0.0).astype(BF16))
                parts_lo.append(jnp.where(here, lo[i : i + 1, :], 0.0).astype(BF16))
            left = jnp.concatenate(
                [jnp.concatenate(parts_hi, axis=1), jnp.concatenate(parts_lo, axis=1)], axis=0
            )
            right = jnp.concatenate([onecol[it * chunk + i] for i in range(chunk)], axis=1)
            both = lax.dot_general(
                left, right, (((1,), (1,)), ((), ())), preferred_element_type=F32
            )
            acc[slot] += both[:rows] + both[rows:]
            return carry

        acc[slot] = jnp.zeros((rows, cols), F32)
        lax.fori_loop(0, steps, step, 0)

    scatter(lambda at: jnp.where(node_ref[at, :] >= 0, cond_ref[at, :], 0.0), 0)
    inverse = 1.0 / (4.0 + shunt_ref[...] + acc[0])

    ids.wait()
    wanted = jnp.concatenate([ids_got[j] for j in range(nd)], axis=0)
    rids_ref[...] = wanted
    planes[...] = jnp.concatenate(split(pkg_ref[...]), axis=1)
    pick_rows(wanted, me * blocks, planes, start_ref)
    for j in range(nd):
        rows_out[j] = start_ref[j * cap : (j + 1) * cap, :]
    rows_x = Exchange(nd, me, rows_out, rows_got, sem_rows.at[0], sem_rows.at[1])
    rows_x.start()

    lane = lax.broadcasted_iota(jnp.int32, (nblk, 128), 1)
    sub = lax.broadcasted_iota(jnp.int32, (nblk, 128), 0)
    mine = jnp.logical_or(lane == sub, lane == sub + 64)
    in_lanes = jnp.sum(jnp.where(mine, wanted.astype(F32), 0.0), axis=0, keepdims=True)

    rows_x.wait()
    for j in range(nd):
        start_ref[j * cap : (j + 1) * cap, :] = rows_got[j]
    scatter(
        lambda at: jnp.where(node_ref[at, :] >= 0, cond_ref[at, :] * start_ref[at, :], 0.0), 1
    )
    right_side = acc[1] - load_ref[...]

    middle = (slice(8, 8 + rows), slice(128, 128 + cols))
    for k, (ext, tile) in enumerate(
        ((vx, volt_ref[...]), (rx, right_side), (dx, inverse))
    ):
        ext[middle] = tile
        for b in range(2):
            side = slice(b * (cols - 128), b * (cols - 128) + 128)
            edge_n[b, 8 * k : 8 * k + 8, :] = tile[:8, side]
            edge_s[b, 8 * k : 8 * k + 8, :] = tile[rows - 8 :, side]
        edge_w[8 * k : 8 * k + 8, :] = jnp.transpose(tile[:, :128])[:8]
        edge_e[8 * k : 8 * k + 8, :] = jnp.transpose(tile[:, cols - 128 :])[120:]
    halos = [
        remote(src, dst, sem_halo.at[0, k], sem_halo.at[1, k], grp=g, die=d)
        for k, (src, dst, g, d) in enumerate(
            (
                (edge_n, halo_s, up, me),
                (edge_s, halo_n, down, me),
                (edge_w, halo_e, mg, west),
                (edge_e, halo_w, mg, east),
                (edge_n.at[0], halo_se, up, west),
                (edge_n.at[1], halo_sw, up, east),
                (edge_s.at[0], halo_ne, down, west),
                (edge_s.at[1], halo_nw, down, east),
            )
        )
    ]
    for copy in halos:
        copy.start()
    for copy in halos:
        copy.wait_recv()
    pad = jnp.zeros((120, 128), F32)
    for k, ext in enumerate((vx, rx, dx)):
        at = slice(8 * k, 8 * k + 8)
        for b in range(2):
            side = slice(128 + b * (cols - 128), 256 + b * (cols - 128))
            ext[0:8, side] = halo_n[b, at, :]
            ext[8 + rows :, side] = halo_s[b, at, :]
        ext[8 : 8 + rows, 0:128] = jnp.transpose(jnp.concatenate([pad, halo_w[at, :]], axis=0))
        ext[8 : 8 + rows, 128 + cols :] = jnp.transpose(
            jnp.concatenate([halo_e[at, :], pad], axis=0)
        )
        ext[0:8, 0:128] = halo_nw[at, :]
        ext[0:8, 128 + cols :] = halo_ne[at, :]
        ext[8 + rows :, 0:128] = halo_sw[at, :]
        ext[8 + rows :, 128 + cols :] = halo_se[at, :]

    height, width = rows + 16, cols + 256
    grow = lax.broadcasted_iota(jnp.int32, (height, width), 0) + (mg * rows - 8)
    gcol = lax.broadcasted_iota(jnp.int32, (height, width), 1) + (me * cols - 128)
    inside = (grow >= 0) & (grow < ng * rows) & (gcol >= 0) & (gcol < nd * cols)
    v = jnp.where(inside, vx[...], 0.0)
    r = rx[...]
    inv = dx[...]
    for weight in sweep_weights(SWEEPS):
        beside = (
            pltpu.roll(v, 1, 0)
            + pltpu.roll(v, height - 1, 0)
            + pltpu.roll(v, 1, 1)
            + pltpu.roll(v, width - 1, 1)
        )
        v = jnp.where(inside, v + weight * ((r + beside) * inv - v), 0.0)
    final = v[middle]
    out_ref[...] = final
    halves = jnp.concatenate(split(final), axis=0)

    def currents(it, carry):
        at = pl.ds(pl.multiple_of(it * chunk, chunk), chunk)
        node = node_ref[at, :]
        row = jnp.right_shift(node, cols.bit_length() - 1)
        right = jnp.concatenate([onecol[it * chunk + i] for i in range(chunk)], axis=1)
        both = jnp.dot(halves, right, preferred_element_type=F32)
        by_row = both[:rows] + both[rows:]
        seen = [
            jnp.sum(
                jnp.where(row_iota == row[i : i + 1, :], by_row[:, 128 * i : 128 * i + 128], 0.0),
                axis=0,
                keepdims=True,
            )
            for i in range(chunk)
        ]
        flow = jnp.where(
            node >= 0, cond_ref[at, :] * (start_ref[at, :] - jnp.concatenate(seen, axis=0)), 0.0
        )
        for i in range(chunk // cap):
            cur_out[it * (chunk // cap) + i] = flow[i * cap : (i + 1) * cap]
        return carry

    lax.fori_loop(0, steps, currents, 0)
    cur_x = Exchange(nd, me, cur_out, cur_got, sem_cur.at[0], sem_cur.at[1])
    cur_x.start()
    cur_x.wait()
    for j in range(nd):
        item_ref[j * cap : (j + 1) * cap, :] = cur_got[j]
    item_ref[nblk:, :] = jnp.broadcast_to(in_lanes, (8, 128))
    for x in (ids, rows_x, cur_x):
        x.drain()
    for copy in halos:
        copy.wait_send()


def pkg_kernel(
    nd, ng, cap, blocks,
    item_ref, rids_ref, pkg_ref, diag_ref, pat_ref, wt_ref, coup_ref,
    plane_ref, bump_ref,
    items, x_f, x_s, inf_x, diag_x, pat_x, wt_x, wmat, acc, rows_out, rows_got,
    sem_const, sem_ring, sem_ring_send, sem_part, sem_core, sem_core_send, sem_inf, sem_rows,
):
    me, mg = lax.axis_index("die"), lax.axis_index("grp")
    ny = ng // 4
    half = ny // 2
    c = lax.rem(mg, 2)
    y = lax.rem(mg // 2, ny)
    h = mg // (2 * ny)
    nblk = rids_ref.shape[0]
    ext = blocks + 256
    tiles = ext // 128

    def index(hh, yy, cc):
        return (hh * ny + yy) * 2 + cc

    plus, minus = lax.rem(y + 1, ny), lax.rem(y + ny - 1, ny)
    west, east = lax.rem(me + nd - 1, nd), lax.rem(me + 1, nd)
    barrier = pltpu.get_barrier_semaphore()
    for k in range(1, nd):
        signal(barrier, die=lax.rem(me + k, nd))
    for g in (index(h, plus, c), index(h, minus, c), index(1 - h, y, c), index(h, y, 1 - c)):
        signal(barrier, grp=g)

    own = pl.ds(128, blocks)
    diag_x[own, :] = 1.0 / diag_ref[...]
    pat_x[:, 128 : 128 + blocks] = pat_ref[...]
    wt_x[:, 128 : 128 + blocks] = wt_ref[...]
    for ref in (x_s,):
        ref[0:64, :] = jnp.zeros((64, 256), BF16)
        ref[64 + ext :, :] = jnp.zeros((64, 256), BF16)
    inf_x[0:32, :] = jnp.zeros((32, 128), F32)
    inf_x[ext - 32 :, :] = jnp.zeros((32, 128), F32)
    items[mg] = item_ref[...]

    def build(t, carry):
        at = pl.ds(pl.multiple_of(t * 128, 128), 128)
        ids = pat_x[:, at] + (128 + 64 - me * blocks - t * 128)
        weights = wt_x[:, at]
        source = lax.broadcasted_iota(jnp.int32, (256, 128), 0)
        total = jnp.zeros((256, 128), F32)
        for k in range(ids.shape[0]):
            total += jnp.where(source == ids[k : k + 1, :], weights[k : k + 1, :], 0.0)
        wmat[t] = jnp.concatenate(split(jnp.transpose(total)), axis=0)
        return carry

    lax.fori_loop(1, tiles - 1, build, 0)
    pl.semaphore_wait(barrier, nd - 1 + 4)

    tail, head = pl.ds(128 + blocks, 128), pl.ds(0, 128)
    first, last = pl.ds(0, 128), pl.ds(blocks - 128, 128)
    lanes_tail, lanes_last = slice(128 + blocks, 256 + blocks), slice(blocks - 128, blocks)

    core = index(h, y, 1 - c)
    part = index(1 - h, y, c)
    right, left = index(h, plus, c), index(h, minus, c)

    def held(dist, k):
        hh = h if k == 0 else 1 - h
        return index(hh, lax.rem(y + ny + dist, ny), c)

    def pass_on(slot, to, direction, dist, k):
        copy = remote(
            items.at[slot],
            items.at[slot],
            sem_ring_send.at[direction, dist, k],
            sem_ring.at[direction, dist, k],
            grp=to,
        )
        copy.start()
        return copy

    def ring_wait(direction, dist, k):
        slot = held(-dist if direction == 0 else dist, k)
        remote(
            items.at[slot],
            items.at[slot],
            sem_ring_send.at[direction, dist, k],
            sem_ring.at[direction, dist, k],
            grp=right if direction == 0 else left,
        ).wait_recv()
        return slot

    sent = []
    core_sent = []

    def to_core(slot):
        n = len(core_sent)
        copy = remote(
            items.at[slot], items.at[slot], sem_core_send.at[n], sem_core.at[n], grp=core
        )
        copy.start()
        core_sent.append(copy)

    reach = {(0, 0): half, (0, 1): half - 1, (1, 0): half - 1, (1, 1): half}
    for direction, to in ((0, right), (1, left)):
        if reach[direction, 0] >= 1:
            sent.append(pass_on(mg, to, direction, 1, 0))
    to_part = remote(items.at[mg], items.at[mg], sem_part.at[0], sem_part.at[1], grp=part)
    to_part.start()
    to_core(mg)
    consts = []
    for k, (src, dst) in enumerate(
        (
            (pkg_ref.at[first], x_f.at[tail]),
            (diag_x.at[pl.ds(128, 128)], diag_x.at[tail]),
            (pat_ref.at[:, 0:128], pat_x.at[:, lanes_tail]),
            (wt_ref.at[:, 0:128], wt_x.at[:, lanes_tail]),
        )
    ):
        consts.append(remote(src, dst, sem_const.at[0, k], sem_const.at[1, k], die=west))
    for k, (src, dst) in enumerate(
        (
            (pkg_ref.at[last], x_f.at[head]),
            (diag_x.at[pl.ds(blocks, 128)], diag_x.at[head]),
            (pat_ref.at[:, lanes_last], pat_x.at[:, 0:128]),
            (wt_ref.at[:, lanes_last], wt_x.at[:, 0:128]),
        )
    ):
        consts.append(remote(src, dst, sem_const.at[0, 4 + k], sem_const.at[1, 4 + k], die=east))
    for copy in consts:
        copy.start()
    to_part.wait_recv()
    for direction, to in ((0, right), (1, left)):
        if reach[direction, 1] >= 1:
            sent.append(pass_on(part, to, direction, 1, 1))
    to_core(part)
    for dist in range(1, half + 1):
        for k in range(2):
            for direction, to in ((0, right), (1, left)):
                if reach[direction, k] >= dist:
                    slot = ring_wait(direction, dist, k)
                    if reach[direction, k] >= dist + 1:
                        sent.append(pass_on(slot, to, direction, dist + 1, k))
                    to_core(slot)

    for copy in consts:
        copy.wait_recv()
    lax.fori_loop(0, 2, lambda i, carry: build(i * (tiles - 1), carry), 0)
    x_s[64 : 64 + 128, :] = jnp.concatenate(split(x_f[0:128, :]), axis=1)
    x_s[64 + 128 : 64 + 128 + blocks, :] = jnp.concatenate(split(pkg_ref[...]), axis=1)
    x_s[64 + 128 + blocks : 64 + ext, :] = jnp.concatenate(split(x_f[128 + blocks :, :]), axis=1)
    for copy in core_sent:
        copy.wait_recv()

    lane = lax.broadcasted_iota(jnp.int32, (1, 128), 1)
    acc[...] = jnp.zeros((blocks, 256), F32)
    pairs = nblk * 2 == 128

    def gather_sum(q, carry):
        target = lax.broadcasted_iota(jnp.int32, (blocks, 128), 0) + me * blocks
        ones, values = [], []
        for p in range(2):
            a, b = items[4 * q + 2 * p], items[4 * q + 2 * p + 1]
            if pairs:
                ids = jnp.where(lane < 64, a[nblk : nblk + 1, :], b[nblk : nblk + 1, :])
                flows = (a[:nblk], b[:nblk])
            else:
                blank = jnp.zeros((64 - nblk, 128), F32)
                ids = jnp.where(lane < 64, a[nblk : nblk + 1, :], b[nblk : nblk + 1, :])
                flows = (a[:nblk], blank, b[:nblk], blank)
            ids = ids.astype(jnp.int32)
            ones.append(jnp.where(target == ids, 1.0, 0.0).astype(BF16))
            values.append(jnp.concatenate(flows, axis=0))
        acc[...] += jnp.dot(
            jnp.concatenate(ones, axis=1),
            jnp.concatenate(split(jnp.concatenate(values, axis=0)), axis=1),
            preferred_element_type=F32,
        )
        return carry

    lax.fori_loop(0, ng // 4, gather_sum, 0)
    inf_x[own, :] = acc[:, :128] + acc[:, 128:]
    infs = [
        remote(
            inf_x.at[pl.ds(128, 96)],
            inf_x.at[pl.ds(128 + blocks, 96)],
            sem_inf.at[0, 0],
            sem_inf.at[1, 0],
            die=west,
        ),
        remote(
            inf_x.at[pl.ds(32 + blocks, 96)],
            inf_x.at[pl.ds(32, 96)],
            sem_inf.at[0, 1],
            sem_inf.at[1, 1],
            die=east,
        ),
    ]
    for copy in infs:
        copy.start()
    coup = jnp.concatenate(split(coup_ref[...]), axis=1)
    for copy in infs:
        copy.wait_recv()

    for iteration in range(ITERS):
        lo_t, hi_t = (0, tiles) if iteration < ITERS - 1 else (1, tiles - 1)

        def tile(t, carry):
            start = pl.multiple_of(t * 128, 128)
            near = jnp.dot(wmat[t], x_s[pl.ds(start, 256), :], preferred_element_type=F32)
            here = x_s[pl.ds(start + 64, 128), :]
            both = jnp.concatenate([here[:, :128], here[:, 128:]], axis=0)
            block = jnp.dot(both, coup, preferred_element_type=F32)
            total = near + block
            total = total[:128] + total[128:]
            coupled = total[:, :128] + total[:, 128:]
            at = pl.ds(start, 128)
            x_f[at, :] = (-inf_x[at, :] - coupled) * diag_x[at, :]
            return carry

        lax.fori_loop(lo_t, hi_t, tile, 0)
        x_s[64 : 64 + ext, :] = jnp.concatenate(split(x_f[...]), axis=1)

    plane_ref[...] = x_f[own, :]
    pick_rows(
        rids_ref[...], me * blocks, x_s.at[pl.ds(64 + 128, blocks)], bump_ref
    )
    for j in range(nd):
        rows_out[j] = bump_ref[j * cap : (j + 1) * cap, :]
    rows_x = Exchange(nd, me, rows_out, rows_got, sem_rows.at[0], sem_rows.at[1])
    rows_x.start()
    rows_x.wait()
    for j in range(nd):
        bump_ref[j * cap : (j + 1) * cap, :] = rows_got[j]
    rows_x.drain()
    for copy in sent + core_sent + [to_part] + consts + infs:
        copy.wait_send()


def local(
    nd, ng,
    die_volt, die_load, die_shunt, bump_node, bump_block, bump_cond,
    pkg_volt, pkg_diag, pkg_pattern, pkg_weight, block_coupling,
):
    nblk = bump_node.shape[0]
    cap = nblk // nd
    blocks = pkg_volt.shape[0]
    rows, cols = die_volt.shape
    ext = blocks + 256
    vmem = pl.BlockSpec(memory_space=pltpu.VMEM)
    dma = pltpu.SemaphoreType.DMA
    ids = jnp.broadcast_to(bump_block.reshape(nd, cap, 1), (nd, cap, 128))
    exchange_f = pltpu.VMEM((nd, cap, 128), F32)
    strip = pltpu.VMEM((24, 128), F32)
    strips = pltpu.VMEM((2, 24, 128), F32)
    wide = pltpu.VMEM((rows + 16, cols + 256), F32)
    die_out, item, rids = pl.pallas_call(
        functools.partial(die_kernel, nd, ng, cap, blocks),
        out_shape=(
            jax.ShapeDtypeStruct((rows, cols), F32),
            jax.ShapeDtypeStruct((nblk + 8, 128), F32),
            jax.ShapeDtypeStruct((nblk, 128), jnp.int32),
        ),
        in_specs=[vmem] * 7,
        out_specs=(vmem,) * 3,
        scratch_shapes=[
            pltpu.VMEM((nd, cap, 128), jnp.int32),
            exchange_f, exchange_f, exchange_f, exchange_f,
            pltpu.VMEM((nblk, 128), F32),
            pltpu.VMEM((blocks, 256), BF16),
            pltpu.VMEM((nblk, cols, 128), BF16),
            pltpu.VMEM((2, rows, cols), F32),
            wide, wide, wide,
            strips, strips, strip, strip,
            strips, strips, strip, strip, strip, strip, strip, strip,
            dma((2, nd)), dma((2, nd)), dma((2, nd)), dma((2, 8)),
        ],
        compiler_params=pltpu.CompilerParams(collective_id=0, has_side_effects=True),
        name="die_round",
    )(die_volt, die_load, die_shunt, bump_node, ids, bump_cond, pkg_volt)
    plane, bump_out = pl.pallas_call(
        functools.partial(pkg_kernel, nd, ng, cap, blocks),
        out_shape=(
            jax.ShapeDtypeStruct((blocks, 128), F32),
            jax.ShapeDtypeStruct((nblk, 128), F32),
        ),
        in_specs=[vmem] * 7,
        out_specs=(vmem,) * 2,
        scratch_shapes=[
            pltpu.VMEM((ng, nblk + 8, 128), F32),
            pltpu.VMEM((ext, 128), F32),
            pltpu.VMEM((ext + 128, 256), BF16),
            pltpu.VMEM((ext, 128), F32),
            pltpu.VMEM((ext, 128), F32),
            pltpu.VMEM((pkg_pattern.shape[0], ext), jnp.int32),
            pltpu.VMEM((pkg_pattern.shape[0], ext), F32),
            pltpu.VMEM((ext // 128, 256, 256), BF16),
            pltpu.VMEM((blocks, 256), F32),
            exchange_f, exchange_f,
            dma((2, 8)),
            dma((2, ng // 8 + 2, 2)),
            dma((2, ng // 8 + 2, 2)),
            dma((2,)),
            dma((ng // 2,)),
            dma((ng // 2,)),
            dma((2, 2)),
            dma((2, nd)),
        ],
        compiler_params=pltpu.CompilerParams(collective_id=1, has_side_effects=True),
        name="package_round",
    )(item, rids, pkg_volt, pkg_diag, pkg_pattern, pkg_weight, block_coupling)
    return die_out, plane, bump_out


def solution(mesh):
    return jax.shard_map(
        functools.partial(local, mesh.shape["die"], mesh.shape["grp"]),
        mesh=mesh,
        in_specs=(
            P("grp", "die"),
            P("grp", "die"),
            P("grp", "die"),
            P(("grp", "die"), None),
            P(("grp", "die")),
            P(("grp", "die"), None),
            P("die", None),
            P("die", None),
            P(None, "die"),
            P(None, "die"),
            P(),
        ),
        out_specs=(P("grp", "die"), P("die", None), P(("grp", "die"), None)),
        check_vma=False,
    )
```

```python
import functools
import math

import jax
import jax.numpy as jnp
from jax import lax
from jax.experimental import pallas as pl
from jax.experimental.pallas import tpu as pltpu
from jax.sharding import PartitionSpec as P

SWEEPS = 4
ITERS = 4
MESH = pl.DeviceIdType.MESH
F32 = jnp.float32
BF16 = jnp.bfloat16


def sweep_weights(sweeps):
    return [
        1.0 / (1.0 + 0.8 * math.cos(math.pi * (2 * index + 1) / (2 * sweeps)))
        for index in range(sweeps)
    ]


def split(x):
    hi = x.astype(BF16)
    lo = (x - hi.astype(F32)).astype(BF16)
    return hi, lo


def remote(src, dst, send_sem, recv_sem, **device):
    return pltpu.make_async_remote_copy(
        src_ref=src,
        dst_ref=dst,
        send_sem=send_sem,
        recv_sem=recv_sem,
        device_id=device,
        device_id_type=MESH,
    )


class Exchange:
    def __init__(self, count, me, src, dst, sems, grp=None):
        self.me = me
        self.src, self.dst = src, dst
        self.copies = []
        for k in range(1 if grp is None else 0, count):
            to = lax.rem(me + k, count)
            where = {"die": to} if grp is None else {"grp": grp, "die": to}
            self.copies.append(
                remote(src.at[to], dst.at[me], sems.at[0, k], sems.at[1, k], **where)
            )

    def start(self):
        for copy in self.copies:
            copy.start()

    def keep(self):
        self.dst[self.me] = self.src[self.me]

    def wait(self):
        for copy in self.copies:
            copy.wait_recv()

    def drain(self):
        for copy in self.copies:
            copy.wait_send()


def kernel(
    nd, ng, cap, blocks,
    block_ref, node_ref, cond_ref,
    volt_hbm, load_hbm, shunt_hbm, pkg_hbm, diag_hbm, pat_hbm, wt_hbm, coup_hbm,
    die_hbm, plane_hbm, bump_hbm,
    volt_ref, load_ref, shunt_ref, coup_ref, die_v, bump_v,
    ids_out, ids_got, rows_out, rows_got, cur_out, cur_got, cur_part,
    start_ref, hot, planes, onecol, acc, vx, rx, dx,
    edge_n, edge_s, edge_w, edge_e,
    halo_n, halo_s, halo_w, halo_e, halo_nw, halo_ne, halo_sw, halo_se,
    redge_n, redge_s, redge_w, redge_e,
    rhalo_n, rhalo_s, rhalo_w, rhalo_e, rhalo_nw, rhalo_ne, rhalo_sw, rhalo_se,
    items, x_f, x_s, inf_x, pkg_x, diag_x, rdiag, pat_x, wt_x, wmat, total,
    sem_in, sem_outs, sem_ids, sem_rows, sem_cur, sem_cur_part, sem_halo, sem_rhalo,
    sem_const, sem_ids_part, sem_ring, sem_core, sem_inf, sem_bump,
):
    me, mg = lax.axis_index("die"), lax.axis_index("grp")
    rows, cols = volt_ref.shape
    nblk = node_ref.shape[0]
    ext = blocks + 256
    tiles = ext // 128
    ny = ng // 4
    half = ny // 2
    c = lax.rem(mg, 2)
    y = lax.rem(mg // 2, ny)
    h = mg // (2 * ny)

    def index(hh, yy, cc):
        return (hh * ny + yy) * 2 + cc

    up, down = lax.rem(mg + ng - 1, ng), lax.rem(mg + 1, ng)
    west, east = lax.rem(me + nd - 1, nd), lax.rem(me + 1, nd)
    plus, minus = lax.rem(y + 1, ny), lax.rem(y + ny - 1, ny)
    right, left = index(h, plus, c), index(h, minus, c)
    core, part = index(h, y, 1 - c), index(1 - h, y, c)

    own = pl.ds(128, blocks)
    own_lanes = slice(128, 128 + blocks)
    loads = [
        pltpu.make_async_copy(src, dst, sem_in.at[k])
        for k, (src, dst) in enumerate(
            (
                (pkg_hbm, pkg_x.at[own]),
                (diag_hbm, diag_x.at[own]),
                (pat_hbm, pat_x.at[:, own_lanes]),
                (wt_hbm, wt_x.at[:, own_lanes]),
                (shunt_hbm, shunt_ref),
                (volt_hbm, volt_ref),
                (load_hbm, load_ref),
                (coup_hbm, coup_ref),
            )
        )
    ]
    for copy in loads:
        copy.start()

    barrier = pltpu.get_barrier_semaphore()

    def signal(**device):
        pl.semaphore_signal(barrier, inc=1, device_id=device, device_id_type=MESH)

    for k in range(1, nd):
        signal(die=lax.rem(me + k, nd))
    for g in (up, down):
        for d in (west, me, east):
            signal(grp=g, die=d)
    for g in (right, left, core):
        signal(grp=g)
    for k in range(nd):
        signal(grp=part, die=lax.rem(me + k, nd))

    for s in range(nblk):
        ids_out[s // cap, s % cap : s % cap + 1, :] = jnp.full((1, 128), block_ref[s], jnp.int32)

    chunk = 8
    steps = nblk // chunk
    shift = cols.bit_length() - 1

    def one_columns(it, carry):
        node = node_ref[pl.ds(pl.multiple_of(it * chunk, chunk), chunk), :]
        col = jnp.bitwise_and(node, cols - 1)
        for i in range(chunk):
            iota = lax.broadcasted_iota(jnp.int32, (cols, 128), 0)
            onecol[it * chunk + i] = jnp.where(iota == col[i : i + 1, :], 1.0, 0.0).astype(BF16)
        return carry

    lax.fori_loop(0, steps, one_columns, 0)
    pl.semaphore_wait(barrier, (nd - 1) + 6 + 3 + nd)

    ids = Exchange(nd, me, ids_out, ids_got, sem_ids)
    ids.start()
    ids.keep()

    for copy in loads[:4]:
        copy.wait()
    tail, head = pl.ds(128 + blocks, 128), pl.ds(0, 128)
    first, last = pl.ds(128, 128), pl.ds(blocks, 128)
    lt, ll = slice(128 + blocks, 256 + blocks), slice(blocks, 128 + blocks)
    lh, lf = slice(0, 128), slice(128, 256)
    consts = [
        remote(src, dst, sem_const.at[0, k], sem_const.at[1, k], die=west if k < 4 else east)
        for k, (src, dst) in enumerate(
            (
                (pkg_x.at[first], pkg_x.at[tail]),
                (diag_x.at[first], diag_x.at[tail]),
                (pat_x.at[:, lf], pat_x.at[:, lt]),
                (wt_x.at[:, lf], wt_x.at[:, lt]),
                (pkg_x.at[last], pkg_x.at[head]),
                (diag_x.at[last], diag_x.at[head]),
                (pat_x.at[:, ll], pat_x.at[:, lh]),
                (wt_x.at[:, ll], wt_x.at[:, lh]),
            )
        )
    ]
    for copy in consts:
        copy.start()

    row_iota = lax.broadcasted_iota(jnp.int32, (rows, 128), 0)

    def scatter(value_of, slot):
        def step(it, carry):
            at = pl.ds(pl.multiple_of(it * chunk, chunk), chunk)
            node = node_ref[at, :]
            row = jnp.right_shift(node, shift)
            hi, lo = [v.astype(F32) for v in split(value_of(at))]
            parts_hi, parts_lo = [], []
            for i in range(chunk):
                here = row_iota == row[i : i + 1, :]
                parts_hi.append(jnp.where(here, hi[i : i + 1, :], 0.0).astype(BF16))
                parts_lo.append(jnp.where(here, lo[i : i + 1, :], 0.0).astype(BF16))
            lhs = jnp.concatenate(
                [jnp.concatenate(parts_hi, axis=1), jnp.concatenate(parts_lo, axis=1)], axis=0
            )
            rhs = jnp.concatenate([onecol[it * chunk + i] for i in range(chunk)], axis=1)
            both = lax.dot_general(
                lhs, rhs, (((1,), (1,)), ((), ())), preferred_element_type=F32
            )
            acc[slot] += both[:rows] + both[rows:]
            return carry

        acc[slot] = jnp.zeros((rows, cols), F32)
        lax.fori_loop(0, steps, step, 0)

    loads[4].wait()
    scatter(lambda at: jnp.where(node_ref[at, :] >= 0, cond_ref[at, :], 0.0), 0)

    def halo_copies(en, es, ew, ee, n, s, w, e, nw, ne, sw, se, sems):
        return [
            remote(src, dst, sems.at[0, k], sems.at[1, k], grp=g, die=d)
            for k, (src, dst, g, d) in enumerate(
                (
                    (en, s, up, me),
                    (es, n, down, me),
                    (ew, e, mg, west),
                    (ee, w, mg, east),
                    (en.at[0], se, up, west),
                    (en.at[1], sw, up, east),
                    (es.at[0], ne, down, west),
                    (es.at[1], nw, down, east),
                )
            )
        ]

    middle = (slice(8, 8 + rows), slice(128, 128 + cols))

    def set_edges(k, ext_ref, tile, en, es, ew, ee):
        at = slice(8 * k, 8 * k + 8)
        ext_ref[middle] = tile
        for b in range(2):
            side = slice(b * (cols - 128), b * (cols - 128) + 128)
            en[b, at, :] = tile[:8, side]
            es[b, at, :] = tile[rows - 8 :, side]
        ew[at, :] = jnp.transpose(tile[:, :128])[:8]
        ee[at, :] = jnp.transpose(tile[:, cols - 128 :])[120:]

    pad = jnp.zeros((120, 128), F32)

    def set_halos(k, ext_ref, n, s, w, e, nw, ne, sw, se):
        at = slice(8 * k, 8 * k + 8)
        for b in range(2):
            side = slice(128 + b * (cols - 128), 256 + b * (cols - 128))
            ext_ref[0:8, side] = n[b, at, :]
            ext_ref[8 + rows :, side] = s[b, at, :]
        ext_ref[8 : 8 + rows, 0:128] = jnp.transpose(jnp.concatenate([pad, w[at, :]], axis=0))
        ext_ref[8 : 8 + rows, 128 + cols :] = jnp.transpose(
            jnp.concatenate([e[at, :], pad], axis=0)
        )
        ext_ref[0:8, 0:128] = nw[at, :]
        ext_ref[0:8, 128 + cols :] = ne[at, :]
        ext_ref[8 + rows :, 0:128] = sw[at, :]
        ext_ref[8 + rows :, 128 + cols :] = se[at, :]

    edges = (edge_n, edge_s, edge_w, edge_e)
    halos = (halo_n, halo_s, halo_w, halo_e, halo_nw, halo_ne, halo_sw, halo_se)
    redges = (redge_n, redge_s, redge_w, redge_e)
    rhalos = (rhalo_n, rhalo_s, rhalo_w, rhalo_e, rhalo_nw, rhalo_ne, rhalo_sw, rhalo_se)

    planes[...] = jnp.concatenate(split(pkg_x[own, :]), axis=1)
    ids.wait()
    wanted = jnp.concatenate([ids_got[j] for j in range(nd)], axis=0)
    near = wanted - (lax.broadcasted_iota(jnp.int32, wanted.shape, 1) + me * blocks)
    for q in range(blocks // 256):
        for p in range(2):
            hot[q, :, 128 * p : 128 * p + 128] = jnp.where(
                near == 256 * q + 128 * p, 1.0, 0.0
            ).astype(BF16)

    def pick_rows(source, offset, into):
        into[...] = jnp.zeros_like(into)

        def step(q, carry):
            at = pl.ds(pl.multiple_of(offset + q * 256, 64), 256)
            both = jnp.dot(hot[q], source[at, :], preferred_element_type=F32)
            into[...] += both[:, :128] + both[:, 128:]
            return carry

        lax.fori_loop(0, blocks // 256, step, 0)

    pick_rows(planes, 0, start_ref)
    for j in range(nd):
        rows_out[j] = start_ref[j * cap : (j + 1) * cap, :]
    rows_x = Exchange(nd, me, rows_out, rows_got, sem_rows)
    rows_x.start()
    rows_x.keep()

    lane = lax.broadcasted_iota(jnp.int32, (nblk, 128), 1)
    sub = lax.broadcasted_iota(jnp.int32, (nblk, 128), 0)
    mine = jnp.logical_or(lane == sub, lane == sub + 64)
    in_lanes = jnp.sum(jnp.where(mine, wanted.astype(F32), 0.0), axis=0, keepdims=True)
    id_rows = pl.ds(nblk, 8)
    items[mg, nblk:, :] = jnp.broadcast_to(in_lanes, (8, 128))
    ids_part = remote(
        items.at[mg, id_rows], items.at[mg, id_rows], sem_ids_part.at[0], sem_ids_part.at[1],
        grp=part,
    )
    ids_part.start()

    loads[5].wait()
    inverse = 1.0 / (4.0 + shunt_ref[...] + acc[0])
    set_edges(0, vx, volt_ref[...], *edges)
    set_edges(1, dx, inverse, *edges)
    early = halo_copies(*edges, *halos, sem_halo)
    for copy in early:
        copy.start()

    def build(t, carry):
        at = pl.ds(pl.multiple_of(t * 128, 128), 128)
        ids_at = pat_x[:, at] + (128 + 64 - me * blocks - t * 128)
        weights = wt_x[:, at]
        source = lax.broadcasted_iota(jnp.int32, (256, 128), 0)
        matrix = jnp.zeros((256, 128), F32)
        for k in range(ids_at.shape[0]):
            matrix += jnp.where(source == ids_at[k : k + 1, :], weights[k : k + 1, :], 0.0)
        wmat[t] = jnp.concatenate(split(jnp.transpose(matrix)), axis=0)
        return carry

    lax.fori_loop(1, tiles - 1, build, 0)

    rows_x.wait()
    for j in range(nd):
        start_ref[j * cap : (j + 1) * cap, :] = rows_got[j]
    scatter(
        lambda at: jnp.where(node_ref[at, :] >= 0, cond_ref[at, :] * start_ref[at, :], 0.0), 1
    )
    loads[6].wait()
    set_edges(0, rx, acc[1] - load_ref[...], *redges)
    late = halo_copies(*redges, *rhalos, sem_rhalo)
    for copy in late:
        copy.start()
    for copy in early:
        copy.wait_recv()
    set_halos(0, vx, *halos)
    set_halos(1, dx, *halos)
    height, width = rows + 16, cols + 256
    grow = lax.broadcasted_iota(jnp.int32, (height, width), 0) + (mg * rows - 8)
    gcol = lax.broadcasted_iota(jnp.int32, (height, width), 1) + (me * cols - 128)
    inside = (grow >= 0) & (grow < ng * rows) & (gcol >= 0) & (gcol < nd * cols)
    v = jnp.where(inside, vx[...], 0.0)
    for copy in late:
        copy.wait_recv()
    set_halos(0, rx, *rhalos)
    r = rx[...]
    inv = dx[...]
    for weight in sweep_weights(SWEEPS):
        beside = (
            pltpu.roll(v, 1, 0)
            + pltpu.roll(v, height - 1, 0)
            + pltpu.roll(v, 1, 1)
            + pltpu.roll(v, width - 1, 1)
        )
        v = jnp.where(inside, v + weight * ((r + beside) * inv - v), 0.0)
    final = v[middle]
    die_v[...] = final
    die_done = pltpu.make_async_copy(die_v, die_hbm, sem_outs.at[0])
    die_done.start()
    halves = jnp.concatenate(split(final), axis=0)

    def currents(it, carry):
        at = pl.ds(pl.multiple_of(it * chunk, chunk), chunk)
        node = node_ref[at, :]
        row = jnp.right_shift(node, shift)
        rhs = jnp.concatenate([onecol[it * chunk + i] for i in range(chunk)], axis=1)
        both = jnp.dot(halves, rhs, preferred_element_type=F32)
        by_row = both[:rows] + both[rows:]
        seen = [
            jnp.sum(
                jnp.where(row_iota == row[i : i + 1, :], by_row[:, 128 * i : 128 * i + 128], 0.0),
                axis=0,
                keepdims=True,
            )
            for i in range(chunk)
        ]
        flow = jnp.where(
            node >= 0, cond_ref[at, :] * (start_ref[at, :] - jnp.concatenate(seen, axis=0)), 0.0
        )
        for i in range(chunk // cap):
            cur_out[it * (chunk // cap) + i] = flow[i * cap : (i + 1) * cap]
        return carry

    lax.fori_loop(0, steps, currents, 0)
    cur_x = Exchange(nd, me, cur_out, cur_got, sem_cur)
    cur_p = Exchange(nd, me, cur_out, cur_part, sem_cur_part, grp=part)
    cur_x.start()
    cur_p.start()
    cur_x.keep()

    for copy in consts:
        copy.wait_recv()
    lax.fori_loop(0, 2, lambda i, carry: build(i * (tiles - 1), carry), 0)
    rdiag[...] = 1.0 / diag_x[...]
    for q in range(ITERS + 1):
        x_s[q, 0:64, :] = jnp.zeros((64, 256), BF16)
        x_s[q, 64 + ext :, :] = jnp.zeros((64, 256), BF16)
    x_s[0, 64 : 64 + ext, :] = jnp.concatenate(split(pkg_x[...]), axis=1)
    inf_x[0:32, :] = jnp.zeros((32, 128), F32)
    inf_x[ext - 32 :, :] = jnp.zeros((32, 128), F32)
    total[...] = jnp.zeros((blocks, 256), F32)
    loads[7].wait()

    sent = []
    core_of = {}

    def pass_on(slot, direction, dist, k):
        copy = remote(
            items.at[slot], items.at[slot],
            sem_ring.at[0, direction, dist, k], sem_ring.at[1, direction, dist, k],
            grp=right if direction == 0 else left,
        )
        copy.start()
        sent.append(copy)

    def to_core(slot, key):
        n = len(core_of)
        copy = remote(
            items.at[slot], items.at[slot], sem_core.at[0, n], sem_core.at[1, n], grp=core
        )
        copy.start()
        core_of[key] = copy

    def held(direction, dist, k, cc):
        yy = lax.rem(y + ny - dist, ny) if direction == 0 else lax.rem(y + dist, ny)
        return index(h if k == 0 else 1 - h, yy, cc)

    reach = {(0, 0): half, (0, 1): half - 1, (1, 0): half - 1, (1, 1): half}
    first_lanes = lax.broadcasted_iota(jnp.int32, (1, 128), 1) < 64

    def add_group(slots):
        def ids_of(slot):
            return items[slot, nblk : nblk + 1, :]

        pair_ids = [
            jnp.where(first_lanes, ids_of(slots[2 * p]), ids_of(slots[2 * p + 1])).astype(
                jnp.int32
            )
            - me * blocks
            for p in range(2)
        ]
        flows = []
        for slot in slots:
            flows.append(items[slot, :nblk, :])
            if nblk < 64:
                flows.append(jnp.zeros((64 - nblk, 128), F32))
        rhs = jnp.concatenate(split(jnp.concatenate(flows, axis=0)), axis=1)
        planes[0:256, :] = rhs

        def step(q, carry):
            at = pl.ds(pl.multiple_of(q * 256, 256), 256)
            target = lax.broadcasted_iota(jnp.int32, (256, 128), 0) + q * 256
            lhs = jnp.concatenate(
                [jnp.where(target == i, 1.0, 0.0).astype(BF16) for i in pair_ids], axis=1
            )
            total[at, :] += jnp.dot(lhs, planes[0:256, :], preferred_element_type=F32)
            return carry

        lax.fori_loop(0, blocks // 256, step, 0)

    def keys_of(dist):
        keys = [
            (direction, dist, k)
            for k in range(2)
            for direction in range(2)
            if reach[direction, k] >= dist
        ]
        return keys + (["own", "part"] if dist == half else [])

    def group(dist, cc):
        slots = []
        for key in keys_of(dist):
            if key == "own":
                slots.append(index(h, y, cc))
            elif key == "part":
                slots.append(index(1 - h, y, cc))
            else:
                slots.append(held(*key, cc))
        return slots

    def core_group(dist):
        for key in keys_of(dist):
            core_of[key].wait_recv()
        add_group(group(dist, 1 - c))

    cur_x.wait()
    for j in range(nd):
        items[mg, j * cap : (j + 1) * cap, :] = cur_got[j]
    for direction in range(2):
        if reach[direction, 0] >= 1:
            pass_on(mg, direction, 1, 0)
    to_core(mg, "own")
    ids_part.wait_recv()
    cur_p.wait()
    for j in range(nd):
        items[part, j * cap : (j + 1) * cap, :] = cur_part[j]
    for direction in range(2):
        if reach[direction, 1] >= 1:
            pass_on(part, direction, 1, 1)
    to_core(part, "part")
    for dist in range(1, half + 1):
        for k in range(2):
            for direction in range(2):
                if reach[direction, k] >= dist:
                    slot = held(direction, dist, k, c)
                    remote(
                        items.at[slot], items.at[slot],
                        sem_ring.at[0, direction, dist, k], sem_ring.at[1, direction, dist, k],
                        grp=right if direction == 0 else left,
                    ).wait_recv()
                    if reach[direction, k] >= dist + 1:
                        pass_on(slot, direction, dist + 1, k)
                    to_core(slot, (direction, dist, k))
        add_group(group(dist, c))
        if dist > 1:
            core_group(dist - 1)
    core_group(half)

    inf_x[own, :] = total[:, :128] + total[:, 128:]
    infs = [
        remote(
            inf_x.at[pl.ds(src, 96)], inf_x.at[pl.ds(dst, 96)],
            sem_inf.at[0, k], sem_inf.at[1, k], die=to,
        )
        for k, (src, dst, to) in enumerate(
            ((128, 128 + blocks, west), (32 + blocks, 32, east))
        )
    ]
    for copy in infs:
        copy.start()
    coup = jnp.concatenate(split(coup_ref[...]), axis=1)

    def tile(iteration, t):
        start = pl.multiple_of(t * 128, 128)
        at = pl.ds(start, 128)
        near = jnp.dot(
            wmat[t], x_s[iteration - 1, pl.ds(start, 256), :], preferred_element_type=F32
        )
        here = x_s[iteration - 1, pl.ds(start + 64, 128), :]
        both = jnp.concatenate([here[:, :128], here[:, 128:]], axis=0)
        coupled = near + jnp.dot(both, coup, preferred_element_type=F32)
        coupled = coupled[:128] + coupled[128:]
        coupled = coupled[:, :128] + coupled[:, 128:]
        value = (-inf_x[at, :] - coupled) * rdiag[at, :]
        if iteration == ITERS:
            x_f[at, :] = value
        x_s[iteration, pl.ds(start + 64, 128), :] = jnp.concatenate(split(value), axis=1)

    def pairs(iteration, begin, end):
        def step(i, carry):
            tile(iteration, i)
            tile(iteration, tiles - 1 - i)
            return carry

        if end > begin:
            lax.fori_loop(begin, end, step, 0)

    deep = tiles // 2
    for iteration in range(1, ITERS + 1):
        pairs(iteration, min(iteration, deep), deep)
    for copy in infs:
        copy.wait_recv()
    for iteration in range(1, ITERS + 1):
        pairs(iteration, 1 if iteration == ITERS else 0, min(iteration, deep))

    plane_done = pltpu.make_async_copy(x_f.at[own], plane_hbm, sem_outs.at[1])
    plane_done.start()
    rows_x.drain()
    pick_rows(x_s.at[ITERS], 64 + 128, start_ref)
    for j in range(nd):
        rows_out[j] = start_ref[j * cap : (j + 1) * cap, :]
    bump_x = Exchange(nd, me, rows_out, rows_got, sem_bump)
    bump_x.start()
    bump_x.keep()
    for x in (ids, cur_x, cur_p):
        x.drain()
    for copy in sent + list(core_of.values()) + [ids_part] + consts + infs + early + late:
        copy.wait_send()
    bump_x.wait()
    for j in range(nd):
        bump_v[j * cap : (j + 1) * cap, :] = rows_got[j]
    bump_done = pltpu.make_async_copy(bump_v, bump_hbm, sem_outs.at[2])
    bump_done.start()
    bump_x.drain()
    die_done.wait()
    plane_done.wait()
    bump_done.wait()


def local(
    nd, ng,
    die_volt, die_load, die_shunt, bump_node, bump_block, bump_cond,
    pkg_volt, pkg_diag, pkg_pattern, pkg_weight, block_coupling,
):
    nblk = bump_node.shape[0]
    cap = nblk // nd
    blocks = pkg_volt.shape[0]
    rows, cols = die_volt.shape
    ext = blocks + 256
    knb = pkg_pattern.shape[0]
    vmem = pl.BlockSpec(memory_space=pltpu.VMEM)
    anywhere = pl.BlockSpec(memory_space=pl.ANY)
    dma = pltpu.SemaphoreType.DMA

    def buf(*shape, dtype=F32):
        return pltpu.VMEM(shape, dtype)

    def strip_set(depth):
        return [
            buf(2, depth, 128), buf(2, depth, 128), buf(depth, 128), buf(depth, 128),
            buf(2, depth, 128), buf(2, depth, 128), buf(depth, 128), buf(depth, 128),
            buf(depth, 128), buf(depth, 128), buf(depth, 128), buf(depth, 128),
        ]

    return pl.pallas_call(
        functools.partial(kernel, nd, ng, cap, blocks),
        out_shape=(
            jax.ShapeDtypeStruct((rows, cols), F32),
            jax.ShapeDtypeStruct((blocks, 128), F32),
            jax.ShapeDtypeStruct((nblk, 128), F32),
        ),
        in_specs=[pl.BlockSpec(memory_space=pltpu.SMEM), vmem, vmem] + [anywhere] * 8,
        out_specs=(anywhere,) * 3,
        scratch_shapes=[
            buf(rows, cols), buf(rows, cols), buf(rows, cols), buf(128, 128),
            buf(rows, cols), buf(nblk, 128),
            buf(nd, cap, 128, dtype=jnp.int32), buf(nd, cap, 128, dtype=jnp.int32),
            buf(nd, cap, 128), buf(nd, cap, 128),
            buf(nd, cap, 128), buf(nd, cap, 128), buf(nd, cap, 128),
            buf(nblk, 128),
            buf(blocks // 256, nblk, 256, dtype=BF16),
            buf(blocks, 256, dtype=BF16),
            buf(nblk, cols, 128, dtype=BF16),
            buf(2, rows, cols),
            buf(rows + 16, cols + 256), buf(rows + 16, cols + 256), buf(rows + 16, cols + 256),
            *strip_set(16),
            *strip_set(8),
            buf(ng, nblk + 8, 128),
            buf(ext, 128),
            buf(ITERS + 1, ext + 128, 256, dtype=BF16),
            buf(ext, 128),
            buf(ext, 128), buf(ext, 128), buf(ext, 128),
            buf(knb, ext, dtype=jnp.int32), buf(knb, ext),
            buf(ext // 128, 256, 256, dtype=BF16),
            buf(blocks, 256),
            dma((8,)), dma((3,)), dma((2, nd)), dma((2, nd)), dma((2, nd)), dma((2, nd)),
            dma((2, 8)), dma((2, 8)), dma((2, 8)), dma((2,)),
            dma((2, 2, ng // 8 + 2, 2)), dma((2, ng // 2)), dma((2, 2)), dma((2, nd)),
        ],
        compiler_params=pltpu.CompilerParams(collective_id=0, has_side_effects=True),
        name="coupling_round",
    )(
        bump_block, bump_node, bump_cond, die_volt, die_load, die_shunt,
        pkg_volt, pkg_diag, pkg_pattern, pkg_weight, block_coupling,
    )


def solution(mesh):
    return jax.shard_map(
        functools.partial(local, mesh.shape["die"], mesh.shape["grp"]),
        mesh=mesh,
        in_specs=(
            P("grp", "die"),
            P("grp", "die"),
            P("grp", "die"),
            P(("grp", "die"), None),
            P(("grp", "die")),
            P(("grp", "die"), None),
            P("die", None),
            P("die", None),
            P(None, "die"),
            P(None, "die"),
            P(),
        ),
        out_specs=(P("grp", "die"), P("die", None), P(("grp", "die"), None)),
        check_vma=False,
    )
```

```python
import functools
import math

import jax
import jax.numpy as jnp
from jax import lax
from jax.experimental import pallas as pl
from jax.experimental.pallas import tpu as pltpu
from jax.sharding import PartitionSpec as P

SWEEPS = 4
ITERS = 4
MESH = pl.DeviceIdType.MESH
F32 = jnp.float32
BF16 = jnp.bfloat16


def sweep_weights(sweeps):
    return [
        1.0 / (1.0 + 0.8 * math.cos(math.pi * (2 * index + 1) / (2 * sweeps)))
        for index in range(sweeps)
    ]


def split(x):
    hi = x.astype(BF16)
    lo = (x - hi.astype(F32)).astype(BF16)
    return hi, lo


def remote(src, dst, send_sem, recv_sem, **device):
    return pltpu.make_async_remote_copy(
        src_ref=src,
        dst_ref=dst,
        send_sem=send_sem,
        recv_sem=recv_sem,
        device_id=device,
        device_id_type=MESH,
    )


class Exchange:
    def __init__(self, count, me, src, dst, sems, grp=None):
        self.me = me
        self.src, self.dst = src, dst
        self.copies = []
        for k in range(1 if grp is None else 0, count):
            to = lax.rem(me + k, count)
            where = {"die": to} if grp is None else {"grp": grp, "die": to}
            self.copies.append(
                remote(src.at[to], dst.at[me], sems.at[0, k], sems.at[1, k], **where)
            )

    def start(self):
        for copy in self.copies:
            copy.start()

    def keep(self):
        self.dst[self.me] = self.src[self.me]

    def wait(self):
        for copy in self.copies:
            copy.wait_recv()

    def drain(self):
        for copy in self.copies:
            copy.wait_send()


def kernel(
    nd, ng, cap, blocks,
    block_ref, node_ref, cond_ref,
    volt_hbm, load_hbm, shunt_hbm, pkg_hbm, diag_hbm, pat_hbm, wt_hbm, coup_hbm,
    die_hbm, plane_hbm, bump_hbm,
    volt_ref, load_ref, shunt_ref, coup_ref, die_v, bump_v,
    ids_out, ids_got, rows_out, rows_got, cur_out, cur_got, cur_part,
    start_ref, hot, planes, onecol, acc, vx, rx, dx,
    edge_n, edge_s, edge_w, edge_e,
    halo_n, halo_s, halo_w, halo_e, halo_nw, halo_ne, halo_sw, halo_se,
    redge_n, redge_s, redge_w, redge_e,
    rhalo_n, rhalo_s, rhalo_w, rhalo_e, rhalo_nw, rhalo_ne, rhalo_sw, rhalo_se,
    items, x_f, x_s, inf_x, pkg_x, diag_x, rdiag, pat_x, wt_x, wmat, total,
    sem_in, sem_outs, sem_ids, sem_rows, sem_cur, sem_cur_part, sem_halo, sem_rhalo,
    sem_const, sem_ids_part, sem_ring, sem_core, sem_inf, sem_bump,
):
    me, mg = lax.axis_index("die"), lax.axis_index("grp")
    rows, cols = volt_ref.shape
    nblk = node_ref.shape[0]
    ext = blocks + 256
    tiles = ext // 128
    ny = ng // 4
    half = ny // 2
    c = lax.rem(mg, 2)
    y = lax.rem(mg // 2, ny)
    h = mg // (2 * ny)

    def index(hh, yy, cc):
        return (hh * ny + yy) * 2 + cc

    up, down = lax.rem(mg + ng - 1, ng), lax.rem(mg + 1, ng)
    west, east = lax.rem(me + nd - 1, nd), lax.rem(me + 1, nd)
    plus, minus = lax.rem(y + 1, ny), lax.rem(y + ny - 1, ny)
    right, left = index(h, plus, c), index(h, minus, c)
    core, part = index(h, y, 1 - c), index(1 - h, y, c)

    own = pl.ds(128, blocks)
    own_lanes = slice(128, 128 + blocks)
    loads = [
        pltpu.make_async_copy(src, dst, sem_in.at[k])
        for k, (src, dst) in enumerate(
            (
                (pkg_hbm, pkg_x.at[own]),
                (diag_hbm, diag_x.at[own]),
                (pat_hbm, pat_x.at[:, own_lanes]),
                (wt_hbm, wt_x.at[:, own_lanes]),
                (shunt_hbm, shunt_ref),
                (volt_hbm, volt_ref),
                (load_hbm, load_ref),
                (coup_hbm, coup_ref),
            )
        )
    ]
    for copy in loads:
        copy.start()

    barrier = pltpu.get_barrier_semaphore()

    def signal(**device):
        pl.semaphore_signal(barrier, inc=1, device_id=device, device_id_type=MESH)

    for k in range(1, nd):
        signal(die=lax.rem(me + k, nd))
    for g in (up, down):
        for d in (west, me, east):
            signal(grp=g, die=d)
    for g in (right, left, core):
        signal(grp=g)
    for k in range(nd):
        signal(grp=part, die=lax.rem(me + k, nd))

    for s in range(nblk):
        ids_out[s // cap, s % cap : s % cap + 1, :] = jnp.full((1, 128), block_ref[s], jnp.int32)

    chunk = 8
    steps = nblk // chunk
    shift = cols.bit_length() - 1

    def one_columns(it, carry):
        node = node_ref[pl.ds(pl.multiple_of(it * chunk, chunk), chunk), :]
        col = jnp.bitwise_and(node, cols - 1)
        for i in range(chunk):
            iota = lax.broadcasted_iota(jnp.int32, (cols, 128), 0)
            onecol[it * chunk + i] = jnp.where(iota == col[i : i + 1, :], 1.0, 0.0).astype(BF16)
        return carry

    lax.fori_loop(0, steps, one_columns, 0)
    pl.semaphore_wait(barrier, (nd - 1) + 6 + 3 + nd)

    ids = Exchange(nd, me, ids_out, ids_got, sem_ids)
    ids.start()
    ids.keep()

    for copy in loads[:4]:
        copy.wait()
    tail, head = pl.ds(128 + blocks, 128), pl.ds(0, 128)
    first, last = pl.ds(128, 128), pl.ds(blocks, 128)
    lt, ll = slice(128 + blocks, 256 + blocks), slice(blocks, 128 + blocks)
    lh, lf = slice(0, 128), slice(128, 256)
    consts = [
        remote(src, dst, sem_const.at[0, k], sem_const.at[1, k], die=west if k < 4 else east)
        for k, (src, dst) in enumerate(
            (
                (pkg_x.at[first], pkg_x.at[tail]),
                (diag_x.at[first], diag_x.at[tail]),
                (pat_x.at[:, lf], pat_x.at[:, lt]),
                (wt_x.at[:, lf], wt_x.at[:, lt]),
                (pkg_x.at[last], pkg_x.at[head]),
                (diag_x.at[last], diag_x.at[head]),
                (pat_x.at[:, ll], pat_x.at[:, lh]),
                (wt_x.at[:, ll], wt_x.at[:, lh]),
            )
        )
    ]
    for copy in consts:
        copy.start()

    row_iota = lax.broadcasted_iota(jnp.int32, (rows, 128), 0)

    def scatter(value_of, slot):
        def step(it, carry):
            at = pl.ds(pl.multiple_of(it * chunk, chunk), chunk)
            node = node_ref[at, :]
            row = jnp.right_shift(node, shift)
            hi, lo = [v.astype(F32) for v in split(value_of(at))]
            parts_hi, parts_lo = [], []
            for i in range(chunk):
                here = row_iota == row[i : i + 1, :]
                parts_hi.append(jnp.where(here, hi[i : i + 1, :], 0.0).astype(BF16))
                parts_lo.append(jnp.where(here, lo[i : i + 1, :], 0.0).astype(BF16))
            lhs = jnp.concatenate(
                [jnp.concatenate(parts_hi, axis=1), jnp.concatenate(parts_lo, axis=1)], axis=0
            )
            rhs = jnp.concatenate([onecol[it * chunk + i] for i in range(chunk)], axis=1)
            both = lax.dot_general(
                lhs, rhs, (((1,), (1,)), ((), ())), preferred_element_type=F32
            )
            acc[slot] += both[:rows] + both[rows:]
            return carry

        acc[slot] = jnp.zeros((rows, cols), F32)

        def double(it, carry):
            step(2 * it, carry)
            return step(2 * it + 1, carry)

        lax.fori_loop(0, steps // 2, double, 0)

    loads[4].wait()
    scatter(lambda at: jnp.where(node_ref[at, :] >= 0, cond_ref[at, :], 0.0), 0)

    def halo_copies(en, es, ew, ee, n, s, w, e, nw, ne, sw, se, sems):
        return [
            remote(src, dst, sems.at[0, k], sems.at[1, k], grp=g, die=d)
            for k, (src, dst, g, d) in enumerate(
                (
                    (en, s, up, me),
                    (es, n, down, me),
                    (ew, e, mg, west),
                    (ee, w, mg, east),
                    (en.at[0], se, up, west),
                    (en.at[1], sw, up, east),
                    (es.at[0], ne, down, west),
                    (es.at[1], nw, down, east),
                )
            )
        ]

    middle = (slice(8, 8 + rows), slice(128, 128 + cols))

    def set_edges(k, ext_ref, tile, en, es, ew, ee):
        at = slice(8 * k, 8 * k + 8)
        ext_ref[middle] = tile
        for b in range(2):
            side = slice(b * (cols - 128), b * (cols - 128) + 128)
            en[b, at, :] = tile[:8, side]
            es[b, at, :] = tile[rows - 8 :, side]
        ew[at, :] = jnp.transpose(tile[:, :128])[:8]
        ee[at, :] = jnp.transpose(tile[:, cols - 128 :])[120:]

    pad = jnp.zeros((120, 128), F32)

    def set_halos(k, ext_ref, n, s, w, e, nw, ne, sw, se):
        at = slice(8 * k, 8 * k + 8)
        for b in range(2):
            side = slice(128 + b * (cols - 128), 256 + b * (cols - 128))
            ext_ref[0:8, side] = n[b, at, :]
            ext_ref[8 + rows :, side] = s[b, at, :]
        ext_ref[8 : 8 + rows, 0:128] = jnp.transpose(jnp.concatenate([pad, w[at, :]], axis=0))
        ext_ref[8 : 8 + rows, 128 + cols :] = jnp.transpose(
            jnp.concatenate([e[at, :], pad], axis=0)
        )
        ext_ref[0:8, 0:128] = nw[at, :]
        ext_ref[0:8, 128 + cols :] = ne[at, :]
        ext_ref[8 + rows :, 0:128] = sw[at, :]
        ext_ref[8 + rows :, 128 + cols :] = se[at, :]

    edges = (edge_n, edge_s, edge_w, edge_e)
    halos = (halo_n, halo_s, halo_w, halo_e, halo_nw, halo_ne, halo_sw, halo_se)
    redges = (redge_n, redge_s, redge_w, redge_e)
    rhalos = (rhalo_n, rhalo_s, rhalo_w, rhalo_e, rhalo_nw, rhalo_ne, rhalo_sw, rhalo_se)

    planes[...] = jnp.concatenate(split(pkg_x[own, :]), axis=1)
    ids.wait()
    wanted = jnp.concatenate([ids_got[j] for j in range(nd)], axis=0)
    near = wanted - (lax.broadcasted_iota(jnp.int32, wanted.shape, 1) + me * blocks)
    for q in range(blocks // 256):
        for p in range(2):
            hot[q, :, 128 * p : 128 * p + 128] = jnp.where(
                near == 256 * q + 128 * p, 1.0, 0.0
            ).astype(BF16)

    def pick_rows(source, offset, into):
        both = jnp.zeros((nblk, 256), F32)
        for q in range(blocks // 256):
            both += jnp.dot(
                hot[q], source[offset + q * 256 : offset + q * 256 + 256, :],
                preferred_element_type=F32,
            )
        into[...] = both[:, :128] + both[:, 128:]

    pick_rows(planes, 0, start_ref)
    for j in range(nd):
        rows_out[j] = start_ref[j * cap : (j + 1) * cap, :]
    rows_x = Exchange(nd, me, rows_out, rows_got, sem_rows)
    rows_x.start()
    rows_x.keep()

    lane = lax.broadcasted_iota(jnp.int32, (nblk, 128), 1)
    sub = lax.broadcasted_iota(jnp.int32, (nblk, 128), 0)
    mine = jnp.logical_or(lane == sub, lane == sub + 64)
    in_lanes = jnp.sum(jnp.where(mine, wanted.astype(F32), 0.0), axis=0, keepdims=True)
    id_rows = pl.ds(nblk, 8)
    items[mg, nblk:, :] = jnp.broadcast_to(in_lanes, (8, 128))
    ids_part = remote(
        items.at[mg, id_rows], items.at[mg, id_rows], sem_ids_part.at[0], sem_ids_part.at[1],
        grp=part,
    )
    ids_part.start()

    loads[5].wait()
    inverse = 1.0 / (4.0 + shunt_ref[...] + acc[0])
    set_edges(0, vx, volt_ref[...], *edges)
    set_edges(1, dx, inverse, *edges)
    early = halo_copies(*edges, *halos, sem_halo)
    for copy in early:
        copy.start()

    def build(t, carry):
        at = pl.ds(pl.multiple_of(t * 128, 128), 128)
        ids_at = pat_x[:, at] + (128 + 64 - me * blocks - t * 128)
        weights = wt_x[:, at]
        source = lax.broadcasted_iota(jnp.int32, (256, 128), 0)
        matrix = jnp.zeros((256, 128), F32)
        for k in range(ids_at.shape[0]):
            matrix += jnp.where(source == ids_at[k : k + 1, :], weights[k : k + 1, :], 0.0)
        wmat[t] = jnp.concatenate(split(jnp.transpose(matrix)), axis=0)
        return carry

    lax.fori_loop(1, tiles - 1, build, 0)

    rows_x.wait()
    for j in range(nd):
        start_ref[j * cap : (j + 1) * cap, :] = rows_got[j]
    scatter(
        lambda at: jnp.where(node_ref[at, :] >= 0, cond_ref[at, :] * start_ref[at, :], 0.0), 1
    )
    loads[6].wait()
    set_edges(0, rx, acc[1] - load_ref[...], *redges)
    late = halo_copies(*redges, *rhalos, sem_rhalo)
    for copy in late:
        copy.start()
    for copy in early:
        copy.wait_recv()
    set_halos(0, vx, *halos)
    set_halos(1, dx, *halos)
    height, width = rows + 16, cols + 256
    grow = lax.broadcasted_iota(jnp.int32, (height, width), 0) + (mg * rows - 8)
    gcol = lax.broadcasted_iota(jnp.int32, (height, width), 1) + (me * cols - 128)
    inside = (grow >= 0) & (grow < ng * rows) & (gcol >= 0) & (gcol < nd * cols)
    v = jnp.where(inside, vx[...], 0.0)
    for copy in late:
        copy.wait_recv()
    set_halos(0, rx, *rhalos)
    r = rx[...]
    inv = dx[...]
    for weight in sweep_weights(SWEEPS):
        beside = (
            pltpu.roll(v, 1, 0)
            + pltpu.roll(v, height - 1, 0)
            + pltpu.roll(v, 1, 1)
            + pltpu.roll(v, width - 1, 1)
        )
        v = jnp.where(inside, v + weight * ((r + beside) * inv - v), 0.0)
    final = v[middle]
    die_v[...] = final
    die_done = pltpu.make_async_copy(die_v, die_hbm, sem_outs.at[0])
    die_done.start()
    halves = jnp.concatenate(split(final), axis=0)

    def currents(it, carry):
        at = pl.ds(pl.multiple_of(it * chunk, chunk), chunk)
        node = node_ref[at, :]
        row = jnp.right_shift(node, shift)
        rhs = jnp.concatenate([onecol[it * chunk + i] for i in range(chunk)], axis=1)
        both = jnp.dot(halves, rhs, preferred_element_type=F32)
        by_row = both[:rows] + both[rows:]
        seen = [
            jnp.sum(
                jnp.where(row_iota == row[i : i + 1, :], by_row[:, 128 * i : 128 * i + 128], 0.0),
                axis=0,
                keepdims=True,
            )
            for i in range(chunk)
        ]
        flow = jnp.where(
            node >= 0, cond_ref[at, :] * (start_ref[at, :] - jnp.concatenate(seen, axis=0)), 0.0
        )
        for i in range(chunk // cap):
            cur_out[it * (chunk // cap) + i] = flow[i * cap : (i + 1) * cap]
        return carry


    def two_currents(it, carry):
        currents(2 * it, carry)
        return currents(2 * it + 1, carry)

    lax.fori_loop(0, steps // 2, two_currents, 0)
    cur_x = Exchange(nd, me, cur_out, cur_got, sem_cur)
    cur_p = Exchange(nd, me, cur_out, cur_part, sem_cur_part, grp=part)
    cur_x.start()
    cur_p.start()
    cur_x.keep()

    for copy in consts:
        copy.wait_recv()
    lax.fori_loop(0, 2, lambda i, carry: build(i * (tiles - 1), carry), 0)
    rdiag[...] = 1.0 / diag_x[...]
    for q in range(ITERS + 1):
        x_s[q, 0:64, :] = jnp.zeros((64, 256), BF16)
        x_s[q, 64 + ext :, :] = jnp.zeros((64, 256), BF16)
    x_s[0, 64 : 64 + ext, :] = jnp.concatenate(split(pkg_x[...]), axis=1)
    inf_x[0:32, :] = jnp.zeros((32, 128), F32)
    inf_x[ext - 32 :, :] = jnp.zeros((32, 128), F32)
    total[...] = jnp.zeros((blocks, 256), F32)
    loads[7].wait()

    sent = []
    core_of = {}

    def pass_on(slot, direction, dist, k):
        copy = remote(
            items.at[slot], items.at[slot],
            sem_ring.at[0, direction, dist, k], sem_ring.at[1, direction, dist, k],
            grp=right if direction == 0 else left,
        )
        copy.start()
        sent.append(copy)

    def to_core(slot, key):
        n = len(core_of)
        copy = remote(
            items.at[slot], items.at[slot], sem_core.at[0, n], sem_core.at[1, n], grp=core
        )
        copy.start()
        core_of[key] = copy

    def held(direction, dist, k, cc):
        yy = lax.rem(y + ny - dist, ny) if direction == 0 else lax.rem(y + dist, ny)
        return index(h if k == 0 else 1 - h, yy, cc)

    reach = {(0, 0): half, (0, 1): half - 1, (1, 0): half - 1, (1, 1): half}
    first_lanes = lax.broadcasted_iota(jnp.int32, (1, 128), 1) < 64

    def add_group(slots):
        def ids_of(slot):
            return items[slot, nblk : nblk + 1, :]

        pair_ids = [
            jnp.where(first_lanes, ids_of(slots[2 * p]), ids_of(slots[2 * p + 1])).astype(
                jnp.int32
            )
            - me * blocks
            for p in range(2)
        ]
        flows = []
        for slot in slots:
            flows.append(items[slot, :nblk, :])
            if nblk < 64:
                flows.append(jnp.zeros((64 - nblk, 128), F32))
        rhs = jnp.concatenate(split(jnp.concatenate(flows, axis=0)), axis=1)
        planes[0:256, :] = rhs

        depth = min(blocks, 512)

        def step(q, carry):
            at = pl.ds(pl.multiple_of(q * depth, depth), depth)
            target = lax.broadcasted_iota(jnp.int32, (depth, 128), 0) + q * depth
            lhs = jnp.concatenate(
                [jnp.where(target == i, 1.0, 0.0).astype(BF16) for i in pair_ids], axis=1
            )
            total[at, :] += jnp.dot(lhs, planes[0:256, :], preferred_element_type=F32)
            return carry

        lax.fori_loop(0, blocks // depth, step, 0)

    def keys_of(dist):
        keys = [
            (direction, dist, k)
            for k in range(2)
            for direction in range(2)
            if reach[direction, k] >= dist
        ]
        return keys + (["own", "part"] if dist == half else [])

    def group(dist, cc):
        slots = []
        for key in keys_of(dist):
            if key == "own":
                slots.append(index(h, y, cc))
            elif key == "part":
                slots.append(index(1 - h, y, cc))
            else:
                slots.append(held(*key, cc))
        return slots

    def core_group(dist):
        for key in keys_of(dist):
            core_of[key].wait_recv()
        add_group(group(dist, 1 - c))

    cur_x.wait()
    for j in range(nd):
        items[mg, j * cap : (j + 1) * cap, :] = cur_got[j]
    for direction in range(2):
        if reach[direction, 0] >= 1:
            pass_on(mg, direction, 1, 0)
    to_core(mg, "own")
    ids_part.wait_recv()
    cur_p.wait()
    for j in range(nd):
        items[part, j * cap : (j + 1) * cap, :] = cur_part[j]
    for direction in range(2):
        if reach[direction, 1] >= 1:
            pass_on(part, direction, 1, 1)
    to_core(part, "part")
    for dist in range(1, half + 1):
        for k in range(2):
            for direction in range(2):
                if reach[direction, k] >= dist:
                    slot = held(direction, dist, k, c)
                    remote(
                        items.at[slot], items.at[slot],
                        sem_ring.at[0, direction, dist, k], sem_ring.at[1, direction, dist, k],
                        grp=right if direction == 0 else left,
                    ).wait_recv()
                    if reach[direction, k] >= dist + 1:
                        pass_on(slot, direction, dist + 1, k)
                    to_core(slot, (direction, dist, k))
        add_group(group(dist, c))
        if dist > 1:
            core_group(dist - 1)
    core_group(half)

    inf_x[own, :] = total[:, :128] + total[:, 128:]
    infs = [
        remote(
            inf_x.at[pl.ds(src, 96)], inf_x.at[pl.ds(dst, 96)],
            sem_inf.at[0, k], sem_inf.at[1, k], die=to,
        )
        for k, (src, dst, to) in enumerate(
            ((128, 128 + blocks, west), (32 + blocks, 32, east))
        )
    ]
    for copy in infs:
        copy.start()
    coup = jnp.concatenate(split(coup_ref[...]), axis=1)

    def tile(iteration, t):
        start = t * 128
        at = pl.ds(start, 128)
        near = jnp.dot(
            wmat[t], x_s[iteration - 1, pl.ds(start, 256), :], preferred_element_type=F32
        )
        here = x_s[iteration - 1, pl.ds(start + 64, 128), :]
        both = jnp.concatenate([here[:, :128], here[:, 128:]], axis=0)
        coupled = near + jnp.dot(both, coup, preferred_element_type=F32)
        coupled = coupled[:128] + coupled[128:]
        coupled = coupled[:, :128] + coupled[:, 128:]
        value = (-inf_x[at, :] - coupled) * rdiag[at, :]
        if iteration == ITERS:
            x_f[at, :] = value
        x_s[iteration, pl.ds(start + 64, 128), :] = jnp.concatenate(split(value), axis=1)

    def pairs(iteration, begin, end):
        for i in range(begin, end):
            tile(iteration, i)
            tile(iteration, tiles - 1 - i)

    deep = tiles // 2
    for iteration in range(1, ITERS + 1):
        pairs(iteration, min(iteration, deep), deep)
    for copy in infs:
        copy.wait_recv()
    for iteration in range(1, ITERS + 1):
        pairs(iteration, 1 if iteration == ITERS else 0, min(iteration, deep))

    plane_done = pltpu.make_async_copy(x_f.at[own], plane_hbm, sem_outs.at[1])
    plane_done.start()
    rows_x.drain()
    pick_rows(x_s.at[ITERS], 64 + 128, start_ref)
    for j in range(nd):
        rows_out[j] = start_ref[j * cap : (j + 1) * cap, :]
    bump_x = Exchange(nd, me, rows_out, rows_got, sem_bump)
    bump_x.start()
    bump_x.keep()
    for x in (ids, cur_x, cur_p):
        x.drain()
    for copy in sent + list(core_of.values()) + [ids_part] + consts + infs + early + late:
        copy.wait_send()
    bump_x.wait()
    for j in range(nd):
        bump_v[j * cap : (j + 1) * cap, :] = rows_got[j]
    bump_done = pltpu.make_async_copy(bump_v, bump_hbm, sem_outs.at[2])
    bump_done.start()
    bump_x.drain()
    die_done.wait()
    plane_done.wait()
    bump_done.wait()


def local(
    nd, ng,
    die_volt, die_load, die_shunt, bump_node, bump_block, bump_cond,
    pkg_volt, pkg_diag, pkg_pattern, pkg_weight, block_coupling,
):
    nblk = bump_node.shape[0]
    cap = nblk // nd
    blocks = pkg_volt.shape[0]
    rows, cols = die_volt.shape
    ext = blocks + 256
    knb = pkg_pattern.shape[0]
    vmem = pl.BlockSpec(memory_space=pltpu.VMEM)
    anywhere = pl.BlockSpec(memory_space=pl.ANY)
    dma = pltpu.SemaphoreType.DMA

    def buf(*shape, dtype=F32):
        return pltpu.VMEM(shape, dtype)

    def strip_set(depth):
        return [
            buf(2, depth, 128), buf(2, depth, 128), buf(depth, 128), buf(depth, 128),
            buf(2, depth, 128), buf(2, depth, 128), buf(depth, 128), buf(depth, 128),
            buf(depth, 128), buf(depth, 128), buf(depth, 128), buf(depth, 128),
        ]

    results = pl.pallas_call(
        functools.partial(kernel, nd, ng, cap, blocks),
        out_shape=(
            jax.ShapeDtypeStruct((rows, cols), F32),
            jax.ShapeDtypeStruct((blocks, 128), F32),
            jax.ShapeDtypeStruct((nblk, 128), F32),
        ),
        in_specs=[pl.BlockSpec(memory_space=pltpu.SMEM), vmem, vmem] + [anywhere] * 8,
        out_specs=(anywhere,) * 3,
        scratch_shapes=[
            buf(rows, cols), buf(rows, cols), buf(rows, cols), buf(128, 128),
            buf(rows, cols), buf(nblk, 128),
            buf(nd, cap, 128, dtype=jnp.int32), buf(nd, cap, 128, dtype=jnp.int32),
            buf(nd, cap, 128), buf(nd, cap, 128),
            buf(nd, cap, 128), buf(nd, cap, 128), buf(nd, cap, 128),
            buf(nblk, 128),
            buf(blocks // 256, nblk, 256, dtype=BF16),
            buf(blocks, 256, dtype=BF16),
            buf(nblk, cols, 128, dtype=BF16),
            buf(2, rows, cols),
            buf(rows + 16, cols + 256), buf(rows + 16, cols + 256), buf(rows + 16, cols + 256),
            *strip_set(16),
            *strip_set(8),
            buf(ng, nblk + 8, 128),
            buf(ext, 128),
            buf(ITERS + 1, ext + 128, 256, dtype=BF16),
            buf(ext, 128),
            buf(ext, 128), buf(ext, 128), buf(ext, 128),
            buf(knb, ext, dtype=jnp.int32), buf(knb, ext),
            buf(ext // 128, 256, 256, dtype=BF16),
            buf(blocks, 256),
            dma((8,)), dma((3,)), dma((2, nd)), dma((2, nd)), dma((2, nd)), dma((2, nd)),
            dma((2, 8)), dma((2, 8)), dma((2, 8)), dma((2,)),
            dma((2, 2, ng // 8 + 2, 2)), dma((2, ng // 2)), dma((2, 2)), dma((2, nd)),
        ],
        compiler_params=pltpu.CompilerParams(collective_id=0, has_side_effects=True),
        name="coupling_round",
    )(
        bump_block, bump_node, bump_cond, die_volt, die_load, die_shunt,
        pkg_volt, pkg_diag, pkg_pattern, pkg_weight, block_coupling,
    )
    return pl.pallas_call(
        hand_over,
        out_shape=tuple(jax.ShapeDtypeStruct(r.shape, F32) for r in results),
        in_specs=[anywhere] * 3,
        out_specs=(anywhere,) * 3,
        scratch_shapes=[buf(*r.shape) for r in results] + [dma((2, 16))],
        name="hand_over",
    )(*results)


def hand_over(*refs):
    sources, targets, held, sem = refs[:3], refs[3:6], refs[6:9], refs[9]
    pieces = []
    for k, (src, dst, mid) in enumerate(zip(sources, targets, held)):
        count = 8 if k == 1 else 2
        depth = src.shape[0] // count
        for p in range(count):
            at = pl.ds(p * depth, depth)
            pieces.append((src.at[at], mid.at[at], dst.at[at]))
    takes = [
        pltpu.make_async_copy(src, mid, sem.at[0, n]) for n, (src, mid, _) in enumerate(pieces)
    ]
    gives = [
        pltpu.make_async_copy(mid, dst, sem.at[1, n]) for n, (_, mid, dst) in enumerate(pieces)
    ]
    for copy in takes:
        copy.start()
    for take, give in zip(takes, gives):
        take.wait()
        give.start()
    for copy in gives:
        copy.wait()


def solution(mesh):
    return jax.shard_map(
        functools.partial(local, mesh.shape["die"], mesh.shape["grp"]),
        mesh=mesh,
        in_specs=(
            P("grp", "die"),
            P("grp", "die"),
            P("grp", "die"),
            P(("grp", "die"), None),
            P(("grp", "die")),
            P(("grp", "die"), None),
            P("die", None),
            P("die", None),
            P(None, "die"),
            P(None, "die"),
            P(),
        ),
        out_specs=(P("grp", "die"), P("die", None), P(("grp", "die"), None)),
        check_vma=False,
    )
```

```python
import functools
import math

import jax
import jax.numpy as jnp
from jax import lax
from jax.experimental import pallas as pl
from jax.experimental.pallas import tpu as pltpu
from jax.sharding import PartitionSpec as P

SWEEPS = 4
ITERS = 4
MESH = pl.DeviceIdType.MESH
F32 = jnp.float32
BF16 = jnp.bfloat16


def sweep_weights(sweeps):
    return [
        1.0 / (1.0 + 0.8 * math.cos(math.pi * (2 * index + 1) / (2 * sweeps)))
        for index in range(sweeps)
    ]


def split(x):
    hi = x.astype(BF16)
    lo = (x - hi.astype(F32)).astype(BF16)
    return hi, lo


def remote(src, dst, send_sem, recv_sem, **device):
    return pltpu.make_async_remote_copy(
        src_ref=src,
        dst_ref=dst,
        send_sem=send_sem,
        recv_sem=recv_sem,
        device_id=device,
        device_id_type=MESH,
    )


class Exchange:
    def __init__(self, count, me, src, dst, sems, grp=None):
        self.me = me
        self.src, self.dst = src, dst
        self.copies = []
        for k in range(1 if grp is None else 0, count):
            to = lax.rem(me + k, count)
            where = {"die": to} if grp is None else {"grp": grp, "die": to}
            self.copies.append(
                remote(src.at[to], dst.at[me], sems.at[0, k], sems.at[1, k], **where)
            )

    def start(self):
        for copy in self.copies:
            copy.start()

    def keep(self):
        self.dst[self.me] = self.src[self.me]

    def wait(self):
        for copy in self.copies:
            copy.wait_recv()

    def drain(self):
        for copy in self.copies:
            copy.wait_send()


def kernel(
    nd, ng, cap, blocks,
    block_hbm, node_hbm, cond_hbm,
    volt_hbm, load_hbm, shunt_hbm, pkg_hbm, diag_hbm, pat_hbm, wt_hbm, coup_hbm,
    die_v, plane_v, bump_v,
    block_ref, node_ref, cond_ref, volt_ref, load_ref, shunt_ref, coup_ref,
    ids_out, ids_got, rows_out, rows_got, cur_out, cur_got, cur_part,
    start_ref, hot, planes, onecol, acc, vx, rx, dx,
    edge_n, edge_s, edge_w, edge_e,
    halo_n, halo_s, halo_w, halo_e, halo_nw, halo_ne, halo_sw, halo_se,
    redge_n, redge_s, redge_w, redge_e,
    rhalo_n, rhalo_s, rhalo_w, rhalo_e, rhalo_nw, rhalo_ne, rhalo_sw, rhalo_se,
    items, x_s, inf_x, pkg_x, diag_x, rdiag, pat_x, wt_x, wmat, total,
    sem_in, sem_ids, sem_rows, sem_cur, sem_cur_part, sem_halo, sem_rhalo,
    sem_const, sem_ids_part, sem_ring, sem_core, sem_inf, sem_bump,
):
    me, mg = lax.axis_index("die"), lax.axis_index("grp")
    rows, cols = volt_ref.shape
    nblk = node_ref.shape[0]
    ext = blocks + 256
    tiles = ext // 128
    ny = ng // 4
    half = ny // 2
    c = lax.rem(mg, 2)
    y = lax.rem(mg // 2, ny)
    h = mg // (2 * ny)

    def index(hh, yy, cc):
        return (hh * ny + yy) * 2 + cc

    up, down = lax.rem(mg + ng - 1, ng), lax.rem(mg + 1, ng)
    west, east = lax.rem(me + nd - 1, nd), lax.rem(me + 1, nd)
    plus, minus = lax.rem(y + 1, ny), lax.rem(y + ny - 1, ny)
    right, left = index(h, plus, c), index(h, minus, c)
    core, part = index(h, y, 1 - c), index(1 - h, y, c)

    barrier = pltpu.get_barrier_semaphore()

    def signal(**device):
        pl.semaphore_signal(barrier, inc=1, device_id=device, device_id_type=MESH)

    for k in range(1, nd):
        signal(die=lax.rem(me + k, nd))
    for g in (up, down):
        for d in (west, me, east):
            signal(grp=g, die=d)
    for g in (right, left, core):
        signal(grp=g)
    for k in range(nd):
        signal(grp=part, die=lax.rem(me + k, nd))

    own = pl.ds(128, blocks)
    own_lanes = slice(128, 128 + blocks)
    loads = [
        pltpu.make_async_copy(src, dst, sem_in.at[k])
        for k, (src, dst) in enumerate(
            (
                (pkg_hbm, pkg_x.at[own]),
                (diag_hbm, diag_x.at[own]),
                (pat_hbm, pat_x.at[:, own_lanes]),
                (wt_hbm, wt_x.at[:, own_lanes]),
                (shunt_hbm, shunt_ref),
                (volt_hbm, volt_ref),
                (load_hbm, load_ref),
                (coup_hbm, coup_ref),
                (node_hbm, node_ref),
                (cond_hbm, cond_ref),
                (block_hbm, block_ref),
            )
        )
    ]
    for copy in loads[::-1]:
        copy.start()
    loads[10].wait()

    for s in range(nblk):
        ids_out[s // cap, s % cap : s % cap + 1, :] = jnp.full((1, 128), block_ref[s], jnp.int32)

    chunk = 8
    steps = nblk // chunk
    shift = cols.bit_length() - 1

    def one_columns(it, carry):
        node = node_ref[pl.ds(pl.multiple_of(it * chunk, chunk), chunk), :]
        col = jnp.bitwise_and(node, cols - 1)
        for i in range(chunk):
            iota = lax.broadcasted_iota(jnp.int32, (cols, 128), 0)
            onecol[it * chunk + i] = jnp.where(iota == col[i : i + 1, :], 1.0, 0.0).astype(BF16)
        return carry

    loads[8].wait()
    lax.fori_loop(0, steps, one_columns, 0)
    pl.semaphore_wait(barrier, (nd - 1) + 6 + 3 + nd)

    ids = Exchange(nd, me, ids_out, ids_got, sem_ids)
    ids.start()
    ids.keep()

    for copy in loads[:4]:
        copy.wait()
    tail, head = pl.ds(128 + blocks, 128), pl.ds(0, 128)
    first, last = pl.ds(128, 128), pl.ds(blocks, 128)
    lt, ll = slice(128 + blocks, 256 + blocks), slice(blocks, 128 + blocks)
    lh, lf = slice(0, 128), slice(128, 256)
    consts = [
        remote(src, dst, sem_const.at[0, k], sem_const.at[1, k], die=west if k < 4 else east)
        for k, (src, dst) in enumerate(
            (
                (pkg_x.at[first], pkg_x.at[tail]),
                (diag_x.at[first], diag_x.at[tail]),
                (pat_x.at[:, lf], pat_x.at[:, lt]),
                (wt_x.at[:, lf], wt_x.at[:, lt]),
                (pkg_x.at[last], pkg_x.at[head]),
                (diag_x.at[last], diag_x.at[head]),
                (pat_x.at[:, ll], pat_x.at[:, lh]),
                (wt_x.at[:, ll], wt_x.at[:, lh]),
            )
        )
    ]
    for copy in consts:
        copy.start()

    row_iota = lax.broadcasted_iota(jnp.int32, (rows, 128), 0)

    def scatter(value_of, slot):
        def step(it, carry):
            at = pl.ds(pl.multiple_of(it * chunk, chunk), chunk)
            node = node_ref[at, :]
            row = jnp.right_shift(node, shift)
            hi, lo = [v.astype(F32) for v in split(value_of(at))]
            parts_hi, parts_lo = [], []
            for i in range(chunk):
                here = row_iota == row[i : i + 1, :]
                parts_hi.append(jnp.where(here, hi[i : i + 1, :], 0.0).astype(BF16))
                parts_lo.append(jnp.where(here, lo[i : i + 1, :], 0.0).astype(BF16))
            lhs = jnp.concatenate(
                [jnp.concatenate(parts_hi, axis=1), jnp.concatenate(parts_lo, axis=1)], axis=0
            )
            rhs = jnp.concatenate([onecol[it * chunk + i] for i in range(chunk)], axis=1)
            both = lax.dot_general(
                lhs, rhs, (((1,), (1,)), ((), ())), preferred_element_type=F32
            )
            acc[slot] += both[:rows] + both[rows:]
            return carry

        acc[slot] = jnp.zeros((rows, cols), F32)

        def double(it, carry):
            step(2 * it, carry)
            return step(2 * it + 1, carry)

        lax.fori_loop(0, steps // 2, double, 0)

    loads[4].wait()
    loads[9].wait()
    scatter(lambda at: jnp.where(node_ref[at, :] >= 0, cond_ref[at, :], 0.0), 0)

    def halo_copies(en, es, ew, ee, n, s, w, e, nw, ne, sw, se, sems):
        return [
            remote(src, dst, sems.at[0, k], sems.at[1, k], grp=g, die=d)
            for k, (src, dst, g, d) in enumerate(
                (
                    (en, s, up, me),
                    (es, n, down, me),
                    (ew, e, mg, west),
                    (ee, w, mg, east),
                    (en.at[0], se, up, west),
                    (en.at[1], sw, up, east),
                    (es.at[0], ne, down, west),
                    (es.at[1], nw, down, east),
                )
            )
        ]

    middle = (slice(8, 8 + rows), slice(128, 128 + cols))

    def set_edges(k, ext_ref, tile, en, es, ew, ee):
        at = slice(8 * k, 8 * k + 8)
        ext_ref[middle] = tile
        for b in range(2):
            side = slice(b * (cols - 128), b * (cols - 128) + 128)
            en[b, at, :] = tile[:8, side]
            es[b, at, :] = tile[rows - 8 :, side]
        ew[at, :] = jnp.transpose(tile[:, :128])[:8]
        ee[at, :] = jnp.transpose(tile[:, cols - 128 :])[120:]

    pad = jnp.zeros((120, 128), F32)

    def set_halos(k, ext_ref, n, s, w, e, nw, ne, sw, se):
        at = slice(8 * k, 8 * k + 8)
        for b in range(2):
            side = slice(128 + b * (cols - 128), 256 + b * (cols - 128))
            ext_ref[0:8, side] = n[b, at, :]
            ext_ref[8 + rows :, side] = s[b, at, :]
        ext_ref[8 : 8 + rows, 0:128] = jnp.transpose(jnp.concatenate([pad, w[at, :]], axis=0))
        ext_ref[8 : 8 + rows, 128 + cols :] = jnp.transpose(
            jnp.concatenate([e[at, :], pad], axis=0)
        )
        ext_ref[0:8, 0:128] = nw[at, :]
        ext_ref[0:8, 128 + cols :] = ne[at, :]
        ext_ref[8 + rows :, 0:128] = sw[at, :]
        ext_ref[8 + rows :, 128 + cols :] = se[at, :]

    edges = (edge_n, edge_s, edge_w, edge_e)
    halos = (halo_n, halo_s, halo_w, halo_e, halo_nw, halo_ne, halo_sw, halo_se)
    redges = (redge_n, redge_s, redge_w, redge_e)
    rhalos = (rhalo_n, rhalo_s, rhalo_w, rhalo_e, rhalo_nw, rhalo_ne, rhalo_sw, rhalo_se)

    planes[...] = jnp.concatenate(split(pkg_x[own, :]), axis=1)
    ids.wait()
    wanted = jnp.concatenate([ids_got[j] for j in range(nd)], axis=0)
    near = wanted - (lax.broadcasted_iota(jnp.int32, wanted.shape, 1) + me * blocks)
    for q in range(blocks // 256):
        for p in range(2):
            hot[q, :, 128 * p : 128 * p + 128] = jnp.where(
                near == 256 * q + 128 * p, 1.0, 0.0
            ).astype(BF16)

    def pick_rows(source, offset, into):
        both = jnp.zeros((nblk, 256), F32)
        for q in range(blocks // 256):
            both += jnp.dot(
                hot[q], source[offset + q * 256 : offset + q * 256 + 256, :],
                preferred_element_type=F32,
            )
        into[...] = both[:, :128] + both[:, 128:]

    pick_rows(planes, 0, start_ref)
    for j in range(nd):
        rows_out[j] = start_ref[j * cap : (j + 1) * cap, :]
    rows_x = Exchange(nd, me, rows_out, rows_got, sem_rows)
    rows_x.start()
    rows_x.keep()

    lane = lax.broadcasted_iota(jnp.int32, (nblk, 128), 1)
    sub = lax.broadcasted_iota(jnp.int32, (nblk, 128), 0)
    mine = jnp.logical_or(lane == sub, lane == sub + 64)
    in_lanes = jnp.sum(jnp.where(mine, wanted.astype(F32), 0.0), axis=0, keepdims=True)
    id_rows = pl.ds(nblk, 8)
    items[mg, nblk:, :] = jnp.broadcast_to(in_lanes, (8, 128))
    ids_part = remote(
        items.at[mg, id_rows], items.at[mg, id_rows], sem_ids_part.at[0], sem_ids_part.at[1],
        grp=part,
    )
    ids_part.start()

    loads[5].wait()
    inverse = 1.0 / (4.0 + shunt_ref[...] + acc[0])
    set_edges(0, vx, volt_ref[...], *edges)
    set_edges(1, dx, inverse, *edges)
    early = halo_copies(*edges, *halos, sem_halo)
    for copy in early:
        copy.start()

    def build(t, carry):
        at = pl.ds(pl.multiple_of(t * 128, 128), 128)
        ids_at = pat_x[:, at] + (128 + 64 - me * blocks - t * 128)
        weights = wt_x[:, at]
        source = lax.broadcasted_iota(jnp.int32, (256, 128), 0)
        matrix = jnp.zeros((256, 128), F32)
        for k in range(ids_at.shape[0]):
            matrix += jnp.where(source == ids_at[k : k + 1, :], weights[k : k + 1, :], 0.0)
        wmat[t] = jnp.concatenate(split(jnp.transpose(matrix)), axis=0)
        return carry

    lax.fori_loop(1, tiles - 1, build, 0)

    rows_x.wait()
    for j in range(nd):
        start_ref[j * cap : (j + 1) * cap, :] = rows_got[j]
    scatter(
        lambda at: jnp.where(node_ref[at, :] >= 0, cond_ref[at, :] * start_ref[at, :], 0.0), 1
    )
    loads[6].wait()
    set_edges(0, rx, acc[1] - load_ref[...], *redges)
    late = halo_copies(*redges, *rhalos, sem_rhalo)
    for copy in late:
        copy.start()
    for copy in early:
        copy.wait_recv()
    set_halos(0, vx, *halos)
    set_halos(1, dx, *halos)
    height, width = rows + 16, cols + 256
    grow = lax.broadcasted_iota(jnp.int32, (height, width), 0) + (mg * rows - 8)
    gcol = lax.broadcasted_iota(jnp.int32, (height, width), 1) + (me * cols - 128)
    inside = (grow >= 0) & (grow < ng * rows) & (gcol >= 0) & (gcol < nd * cols)
    v = jnp.where(inside, vx[...], 0.0)
    for copy in late:
        copy.wait_recv()
    set_halos(0, rx, *rhalos)
    r = rx[...]
    inv = dx[...]
    for weight in sweep_weights(SWEEPS):
        beside = (
            pltpu.roll(v, 1, 0)
            + pltpu.roll(v, height - 1, 0)
            + pltpu.roll(v, 1, 1)
            + pltpu.roll(v, width - 1, 1)
        )
        v = jnp.where(inside, v + weight * ((r + beside) * inv - v), 0.0)
    final = v[middle]
    die_v[...] = final
    halves = jnp.concatenate(split(final), axis=0)

    def currents(it, carry):
        at = pl.ds(pl.multiple_of(it * chunk, chunk), chunk)
        node = node_ref[at, :]
        row = jnp.right_shift(node, shift)
        rhs = jnp.concatenate([onecol[it * chunk + i] for i in range(chunk)], axis=1)
        both = jnp.dot(halves, rhs, preferred_element_type=F32)
        by_row = both[:rows] + both[rows:]
        seen = [
            jnp.sum(
                jnp.where(row_iota == row[i : i + 1, :], by_row[:, 128 * i : 128 * i + 128], 0.0),
                axis=0,
                keepdims=True,
            )
            for i in range(chunk)
        ]
        flow = jnp.where(
            node >= 0, cond_ref[at, :] * (start_ref[at, :] - jnp.concatenate(seen, axis=0)), 0.0
        )
        for i in range(chunk // cap):
            cur_out[it * (chunk // cap) + i] = flow[i * cap : (i + 1) * cap]
        return carry


    def two_currents(it, carry):
        currents(2 * it, carry)
        return currents(2 * it + 1, carry)

    lax.fori_loop(0, steps // 2, two_currents, 0)
    cur_x = Exchange(nd, me, cur_out, cur_got, sem_cur)
    cur_p = Exchange(nd, me, cur_out, cur_part, sem_cur_part, grp=part)
    cur_x.start()
    cur_p.start()
    cur_x.keep()

    for copy in consts:
        copy.wait_recv()
    lax.fori_loop(0, 2, lambda i, carry: build(i * (tiles - 1), carry), 0)
    rdiag[...] = 1.0 / diag_x[...]
    for q in range(ITERS + 1):
        x_s[q, 0:64, :] = jnp.zeros((64, 256), BF16)
        x_s[q, 64 + ext :, :] = jnp.zeros((64, 256), BF16)
    x_s[0, 64 : 64 + ext, :] = jnp.concatenate(split(pkg_x[...]), axis=1)
    inf_x[0:32, :] = jnp.zeros((32, 128), F32)
    inf_x[ext - 32 :, :] = jnp.zeros((32, 128), F32)
    total[...] = jnp.zeros((blocks, 256), F32)
    loads[7].wait()

    sent = []
    core_of = {}

    def pass_on(slot, direction, dist, k):
        copy = remote(
            items.at[slot], items.at[slot],
            sem_ring.at[0, direction, dist, k], sem_ring.at[1, direction, dist, k],
            grp=right if direction == 0 else left,
        )
        copy.start()
        sent.append(copy)

    def to_core(slot, key):
        n = len(core_of)
        copy = remote(
            items.at[slot], items.at[slot], sem_core.at[0, n], sem_core.at[1, n], grp=core
        )
        copy.start()
        core_of[key] = copy

    def held(direction, dist, k, cc):
        yy = lax.rem(y + ny - dist, ny) if direction == 0 else lax.rem(y + dist, ny)
        return index(h if k == 0 else 1 - h, yy, cc)

    reach = {(0, 0): half, (0, 1): half - 1, (1, 0): half - 1, (1, 1): half}
    first_lanes = lax.broadcasted_iota(jnp.int32, (1, 128), 1) < 64

    def add_group(slots):
        def ids_of(slot):
            return items[slot, nblk : nblk + 1, :]

        pair_ids = [
            jnp.where(first_lanes, ids_of(slots[2 * p]), ids_of(slots[2 * p + 1])).astype(
                jnp.int32
            )
            - me * blocks
            for p in range(2)
        ]
        flows = []
        for slot in slots:
            flows.append(items[slot, :nblk, :])
            if nblk < 64:
                flows.append(jnp.zeros((64 - nblk, 128), F32))
        rhs = jnp.concatenate(split(jnp.concatenate(flows, axis=0)), axis=1)
        target = lax.broadcasted_iota(jnp.int32, (blocks, 128), 0)
        lhs = jnp.concatenate(
            [jnp.where(target == i, 1.0, 0.0).astype(BF16) for i in pair_ids], axis=1
        )
        total[...] += jnp.dot(lhs, rhs, preferred_element_type=F32)

    def keys_of(dist):
        keys = [
            (direction, dist, k)
            for k in range(2)
            for direction in range(2)
            if reach[direction, k] >= dist
        ]
        return keys + (["own", "part"] if dist == half else [])

    def group(dist, cc):
        slots = []
        for key in keys_of(dist):
            if key == "own":
                slots.append(index(h, y, cc))
            elif key == "part":
                slots.append(index(1 - h, y, cc))
            else:
                slots.append(held(*key, cc))
        return slots

    def core_group(dist):
        for key in keys_of(dist):
            core_of[key].wait_recv()
        add_group(group(dist, 1 - c))

    cur_x.wait()
    for j in range(nd):
        items[mg, j * cap : (j + 1) * cap, :] = cur_got[j]
    for direction in range(2):
        if reach[direction, 0] >= 1:
            pass_on(mg, direction, 1, 0)
    to_core(mg, "own")
    ids_part.wait_recv()
    cur_p.wait()
    for j in range(nd):
        items[part, j * cap : (j + 1) * cap, :] = cur_part[j]
    for direction in range(2):
        if reach[direction, 1] >= 1:
            pass_on(part, direction, 1, 1)
    to_core(part, "part")
    for dist in range(1, half + 1):
        for k in range(2):
            for direction in range(2):
                if reach[direction, k] >= dist:
                    slot = held(direction, dist, k, c)
                    remote(
                        items.at[slot], items.at[slot],
                        sem_ring.at[0, direction, dist, k], sem_ring.at[1, direction, dist, k],
                        grp=right if direction == 0 else left,
                    ).wait_recv()
                    if reach[direction, k] >= dist + 1:
                        pass_on(slot, direction, dist + 1, k)
                    to_core(slot, (direction, dist, k))
        add_group(group(dist, c))
        if dist > 1:
            core_group(dist - 1)
    core_group(half)

    inf_x[own, :] = total[:, :128] + total[:, 128:]
    infs = [
        remote(
            inf_x.at[pl.ds(src, 96)], inf_x.at[pl.ds(dst, 96)],
            sem_inf.at[0, k], sem_inf.at[1, k], die=to,
        )
        for k, (src, dst, to) in enumerate(
            ((128, 128 + blocks, west), (32 + blocks, 32, east))
        )
    ]
    for copy in infs:
        copy.start()
    coup = jnp.concatenate(split(coup_ref[...]), axis=1)

    def tile(iteration, t):
        start = t * 128
        at = pl.ds(start, 128)
        near = jnp.dot(
            wmat[t], x_s[iteration - 1, pl.ds(start, 256), :], preferred_element_type=F32
        )
        here = x_s[iteration - 1, pl.ds(start + 64, 128), :]
        both = jnp.concatenate([here[:, :128], here[:, 128:]], axis=0)
        coupled = near + jnp.dot(both, coup, preferred_element_type=F32)
        coupled = coupled[:128] + coupled[128:]
        coupled = coupled[:, :128] + coupled[:, 128:]
        value = (-inf_x[at, :] - coupled) * rdiag[at, :]
        if iteration == ITERS:
            plane_v[start - 128 : start, :] = value
        x_s[iteration, pl.ds(start + 64, 128), :] = jnp.concatenate(split(value), axis=1)

    def pairs(iteration, begin, end):
        for i in range(begin, end):
            tile(iteration, i)
            tile(iteration, tiles - 1 - i)

    deep = tiles // 2
    for iteration in range(1, ITERS + 1):
        pairs(iteration, min(iteration, deep), deep)
    for copy in infs:
        copy.wait_recv()
    for iteration in range(1, ITERS + 1):
        pairs(iteration, 1 if iteration == ITERS else 0, min(iteration, deep))

    rows_x.drain()
    pick_rows(x_s.at[ITERS], 64 + 128, start_ref)
    for j in range(nd):
        rows_out[j] = start_ref[j * cap : (j + 1) * cap, :]
    bump_x = Exchange(nd, me, rows_out, rows_got, sem_bump)
    bump_x.start()
    bump_x.keep()
    for x in (ids, cur_x, cur_p):
        x.drain()
    for copy in sent + list(core_of.values()) + [ids_part] + consts + infs + early + late:
        copy.wait_send()
    bump_x.wait()
    for j in range(nd):
        bump_v[j * cap : (j + 1) * cap, :] = rows_got[j]
    bump_x.drain()


def local(
    nd, ng,
    die_volt, die_load, die_shunt, bump_node, bump_block, bump_cond,
    pkg_volt, pkg_diag, pkg_pattern, pkg_weight, block_coupling,
):
    nblk = bump_node.shape[0]
    cap = nblk // nd
    blocks = pkg_volt.shape[0]
    rows, cols = die_volt.shape
    ext = blocks + 256
    knb = pkg_pattern.shape[0]
    anywhere = pl.BlockSpec(memory_space=pl.ANY)
    dma = pltpu.SemaphoreType.DMA

    def buf(*shape, dtype=F32):
        return pltpu.VMEM(shape, dtype)

    def strip_set(depth):
        return [
            buf(2, depth, 128), buf(2, depth, 128), buf(depth, 128), buf(depth, 128),
            buf(2, depth, 128), buf(2, depth, 128), buf(depth, 128), buf(depth, 128),
            buf(depth, 128), buf(depth, 128), buf(depth, 128), buf(depth, 128),
        ]

    results = pl.pallas_call(
        functools.partial(kernel, nd, ng, cap, blocks),
        out_shape=(
            pltpu.VMEM((rows, cols), F32),
            pltpu.VMEM((blocks, 128), F32),
            pltpu.VMEM((nblk, 128), F32),
        ),
        in_specs=[anywhere] * 11,
        out_specs=(pl.BlockSpec(memory_space=pltpu.VMEM),) * 3,
        scratch_shapes=[
            pltpu.SMEM((nblk,), jnp.int32), buf(nblk, 128, dtype=jnp.int32), buf(nblk, 128),
            buf(rows, cols), buf(rows, cols), buf(rows, cols), buf(128, 128),
            buf(nd, cap, 128, dtype=jnp.int32), buf(nd, cap, 128, dtype=jnp.int32),
            buf(nd, cap, 128), buf(nd, cap, 128),
            buf(nd, cap, 128), buf(nd, cap, 128), buf(nd, cap, 128),
            buf(nblk, 128),
            buf(blocks // 256, nblk, 256, dtype=BF16),
            buf(blocks, 256, dtype=BF16),
            buf(nblk, cols, 128, dtype=BF16),
            buf(2, rows, cols),
            buf(rows + 16, cols + 256), buf(rows + 16, cols + 256), buf(rows + 16, cols + 256),
            *strip_set(16),
            *strip_set(8),
            buf(ng, nblk + 8, 128),
            buf(ITERS + 1, ext + 128, 256, dtype=BF16),
            buf(ext, 128),
            buf(ext, 128), buf(ext, 128), buf(ext, 128),
            buf(knb, ext, dtype=jnp.int32), buf(knb, ext),
            buf(ext // 128, 256, 256, dtype=BF16),
            buf(blocks, 256),
            dma((11,)), dma((2, nd)), dma((2, nd)), dma((2, nd)), dma((2, nd)),
            dma((2, 8)), dma((2, 8)), dma((2, 8)), dma((2,)),
            dma((2, 2, ng // 8 + 2, 2)), dma((2, ng // 2)), dma((2, 2)), dma((2, nd)),
        ],
        compiler_params=pltpu.CompilerParams(collective_id=0, has_side_effects=True),
        name="coupling_round",
    )(
        bump_block, bump_node, bump_cond, die_volt, die_load, die_shunt,
        pkg_volt, pkg_diag, pkg_pattern, pkg_weight, block_coupling,
    )
    return pl.pallas_call(
        hand_over,
        out_shape=tuple(jax.ShapeDtypeStruct(r.shape, F32) for r in results),
        in_specs=[pl.BlockSpec(memory_space=pltpu.VMEM)] * 3,
        out_specs=(anywhere,) * 3,
        scratch_shapes=[dma((16,))],
        name="hand_over",
    )(*[pltpu.with_memory_space_constraint(r, pltpu.VMEM) for r in results])


def hand_over(*refs):
    sources, targets, sem = refs[:3], refs[3:6], refs[6]
    copies = []
    for k, (src, dst) in enumerate(zip(sources, targets)):
        count = 8 if k == 1 else 2
        depth = src.shape[0] // count
        for p in range(count):
            at = pl.ds(p * depth, depth)
            copies.append(pltpu.make_async_copy(src.at[at], dst.at[at], sem.at[len(copies)]))
    for copy in copies:
        copy.start()
    for copy in copies:
        copy.wait()


def solution(mesh):
    return jax.shard_map(
        functools.partial(local, mesh.shape["die"], mesh.shape["grp"]),
        mesh=mesh,
        in_specs=(
            P("grp", "die"),
            P("grp", "die"),
            P("grp", "die"),
            P(("grp", "die"), None),
            P(("grp", "die")),
            P(("grp", "die"), None),
            P("die", None),
            P("die", None),
            P(None, "die"),
            P(None, "die"),
            P(),
        ),
        out_specs=(P("grp", "die"), P("die", None), P(("grp", "die"), None)),
        check_vma=False,
    )
```

```python
import functools
import math

import jax
import jax.numpy as jnp
from jax import lax
from jax.experimental import pallas as pl
from jax.experimental.pallas import tpu as pltpu
from jax.sharding import PartitionSpec as P

SWEEPS = 4
ITERS = 4
MESH = pl.DeviceIdType.MESH
F32 = jnp.float32
BF16 = jnp.bfloat16


def sweep_weights(sweeps):
    return [
        1.0 / (1.0 + 0.8 * math.cos(math.pi * (2 * index + 1) / (2 * sweeps)))
        for index in range(sweeps)
    ]


def split(x):
    hi = x.astype(BF16)
    lo = (x - hi.astype(F32)).astype(BF16)
    return hi, lo


def remote(src, dst, send_sem, recv_sem, **device):
    return pltpu.make_async_remote_copy(
        src_ref=src,
        dst_ref=dst,
        send_sem=send_sem,
        recv_sem=recv_sem,
        device_id=device,
        device_id_type=MESH,
    )


class Exchange:
    def __init__(self, count, me, src, dst, sems, grp=None):
        self.me = me
        self.src, self.dst = src, dst
        self.copies = []
        for k in range(1 if grp is None else 0, count):
            to = lax.rem(me + k, count)
            where = {"die": to} if grp is None else {"grp": grp, "die": to}
            self.copies.append(
                remote(src.at[to], dst.at[me], sems.at[0, k], sems.at[1, k], **where)
            )

    def start(self):
        for copy in self.copies:
            copy.start()

    def keep(self):
        self.dst[self.me] = self.src[self.me]

    def wait(self):
        for copy in self.copies:
            copy.wait_recv()

    def drain(self):
        for copy in self.copies:
            copy.wait_send()


def kernel(
    nd, ng, cap, blocks,
    block_hbm, node_hbm, cond_hbm,
    volt_hbm, load_hbm, shunt_hbm, pkg_hbm, diag_hbm, pat_hbm, wt_hbm, coup_hbm,
    die_v, plane_v, bump_v,
    block_ref, node_ref, cond_ref, volt_ref, load_ref, shunt_ref, coup_ref,
    ids_out, ids_got, rows_out, rows_got, cur_out, cur_got, cur_part,
    start_ref, hot, planes, onecol, acc, vx, rx, dx,
    edge_n, edge_s, edge_w, edge_e,
    halo_n, halo_s, halo_w, halo_e, halo_nw, halo_ne, halo_sw, halo_se,
    redge_n, redge_s, redge_w, redge_e,
    rhalo_n, rhalo_s, rhalo_w, rhalo_e, rhalo_nw, rhalo_ne, rhalo_sw, rhalo_se,
    items, x_s, inf_x, pkg_x, diag_x, rdiag, pat_x, wt_x, wmat, total,
    sem_in, sem_ids, sem_rows, sem_cur, sem_cur_part, sem_halo, sem_rhalo,
    sem_const, sem_ids_part, sem_ring, sem_core, sem_inf, sem_bump,
):
    me, mg = lax.axis_index("die"), lax.axis_index("grp")
    rows, cols = volt_ref.shape
    nblk = node_ref.shape[0]
    ext = blocks + 256
    tiles = ext // 128
    ny = ng // 4
    half = ny // 2
    c = lax.rem(mg, 2)
    y = lax.rem(mg // 2, ny)
    h = mg // (2 * ny)

    def index(hh, yy, cc):
        return (hh * ny + yy) * 2 + cc

    up, down = lax.rem(mg + ng - 1, ng), lax.rem(mg + 1, ng)
    west, east = lax.rem(me + nd - 1, nd), lax.rem(me + 1, nd)
    plus, minus = lax.rem(y + 1, ny), lax.rem(y + ny - 1, ny)
    right, left = index(h, plus, c), index(h, minus, c)
    core, part = index(h, y, 1 - c), index(1 - h, y, c)

    barrier = pltpu.get_barrier_semaphore()

    def signal(**device):
        pl.semaphore_signal(barrier, inc=1, device_id=device, device_id_type=MESH)

    for k in range(1, nd):
        signal(die=lax.rem(me + k, nd))
    for g in (up, down):
        for d in (west, me, east):
            signal(grp=g, die=d)
    for g in (
        right, left, core,
        index(h, lax.rem(y + 2, ny), c),
        index(h, lax.rem(y + ny - 2, ny), c),
    ):
        signal(grp=g)
    for k in range(nd):
        signal(grp=part, die=lax.rem(me + k, nd))

    own = pl.ds(128, blocks)
    own_lanes = slice(128, 128 + blocks)
    loads = [
        pltpu.make_async_copy(src, dst, sem_in.at[k])
        for k, (src, dst) in enumerate(
            (
                (pkg_hbm, pkg_x.at[own]),
                (diag_hbm, diag_x.at[own]),
                (pat_hbm, pat_x.at[:, own_lanes]),
                (wt_hbm, wt_x.at[:, own_lanes]),
                (shunt_hbm, shunt_ref),
                (volt_hbm, volt_ref),
                (load_hbm, load_ref),
                (coup_hbm, coup_ref),
                (node_hbm, node_ref),
                (cond_hbm, cond_ref),
                (block_hbm, block_ref),
            )
        )
    ]
    for copy in loads[::-1]:
        copy.start()
    loads[10].wait()

    for s in range(nblk):
        ids_out[s // cap, s % cap : s % cap + 1, :] = jnp.full((1, 128), block_ref[s], jnp.int32)

    chunk = 8
    steps = nblk // chunk
    shift = cols.bit_length() - 1

    def one_columns(it, carry):
        node = node_ref[pl.ds(pl.multiple_of(it * chunk, chunk), chunk), :]
        col = jnp.bitwise_and(node, cols - 1)
        for i in range(chunk):
            iota = lax.broadcasted_iota(jnp.int32, (cols, 128), 0)
            onecol[it * chunk + i] = jnp.where(iota == col[i : i + 1, :], 1.0, 0.0).astype(BF16)
        return carry

    loads[8].wait()
    lax.fori_loop(0, steps, one_columns, 0)
    pl.semaphore_wait(barrier, (nd - 1) + 6 + 5 + nd)

    ids = Exchange(nd, me, ids_out, ids_got, sem_ids)
    ids.start()
    ids.keep()

    for copy in loads[:4]:
        copy.wait()
    tail, head = pl.ds(128 + blocks, 128), pl.ds(0, 128)
    first, last = pl.ds(128, 128), pl.ds(blocks, 128)
    lt, ll = slice(128 + blocks, 256 + blocks), slice(blocks, 128 + blocks)
    lh, lf = slice(0, 128), slice(128, 256)
    consts = [
        remote(src, dst, sem_const.at[0, k], sem_const.at[1, k], die=west if k < 4 else east)
        for k, (src, dst) in enumerate(
            (
                (pkg_x.at[first], pkg_x.at[tail]),
                (diag_x.at[first], diag_x.at[tail]),
                (pat_x.at[:, lf], pat_x.at[:, lt]),
                (wt_x.at[:, lf], wt_x.at[:, lt]),
                (pkg_x.at[last], pkg_x.at[head]),
                (diag_x.at[last], diag_x.at[head]),
                (pat_x.at[:, ll], pat_x.at[:, lh]),
                (wt_x.at[:, ll], wt_x.at[:, lh]),
            )
        )
    ]
    for copy in consts:
        copy.start()

    row_iota = lax.broadcasted_iota(jnp.int32, (rows, 128), 0)

    def scatter(value_of, slot):
        def step(it, carry):
            at = pl.ds(pl.multiple_of(it * chunk, chunk), chunk)
            node = node_ref[at, :]
            row = jnp.right_shift(node, shift)
            hi, lo = [v.astype(F32) for v in split(value_of(at))]
            parts_hi, parts_lo = [], []
            for i in range(chunk):
                here = row_iota == row[i : i + 1, :]
                parts_hi.append(jnp.where(here, hi[i : i + 1, :], 0.0).astype(BF16))
                parts_lo.append(jnp.where(here, lo[i : i + 1, :], 0.0).astype(BF16))
            lhs = jnp.concatenate(
                [jnp.concatenate(parts_hi, axis=1), jnp.concatenate(parts_lo, axis=1)], axis=0
            )
            rhs = jnp.concatenate([onecol[it * chunk + i] for i in range(chunk)], axis=1)
            both = lax.dot_general(
                lhs, rhs, (((1,), (1,)), ((), ())), preferred_element_type=F32
            )
            acc[slot] += both[:rows] + both[rows:]
            return carry

        acc[slot] = jnp.zeros((rows, cols), F32)

        def double(it, carry):
            step(2 * it, carry)
            return step(2 * it + 1, carry)

        lax.fori_loop(0, steps // 2, double, 0)

    loads[4].wait()
    loads[9].wait()
    scatter(lambda at: jnp.where(node_ref[at, :] >= 0, cond_ref[at, :], 0.0), 0)

    def halo_copies(en, es, ew, ee, n, s, w, e, nw, ne, sw, se, sems):
        return [
            remote(src, dst, sems.at[0, k], sems.at[1, k], grp=g, die=d)
            for k, (src, dst, g, d) in enumerate(
                (
                    (en, s, up, me),
                    (es, n, down, me),
                    (ew, e, mg, west),
                    (ee, w, mg, east),
                    (en.at[0], se, up, west),
                    (en.at[1], sw, up, east),
                    (es.at[0], ne, down, west),
                    (es.at[1], nw, down, east),
                )
            )
        ]

    middle = (slice(8, 8 + rows), slice(128, 128 + cols))

    def set_edges(k, ext_ref, tile, en, es, ew, ee):
        at = slice(8 * k, 8 * k + 8)
        ext_ref[middle] = tile
        for b in range(2):
            side = slice(b * (cols - 128), b * (cols - 128) + 128)
            en[b, at, :] = tile[:8, side]
            es[b, at, :] = tile[rows - 8 :, side]
        ew[at, :] = jnp.transpose(tile[:, :128])[:8]
        ee[at, :] = jnp.transpose(tile[:, cols - 128 :])[120:]

    pad = jnp.zeros((120, 128), F32)

    def set_halos(k, ext_ref, n, s, w, e, nw, ne, sw, se):
        at = slice(8 * k, 8 * k + 8)
        for b in range(2):
            side = slice(128 + b * (cols - 128), 256 + b * (cols - 128))
            ext_ref[0:8, side] = n[b, at, :]
            ext_ref[8 + rows :, side] = s[b, at, :]
        ext_ref[8 : 8 + rows, 0:128] = jnp.transpose(jnp.concatenate([pad, w[at, :]], axis=0))
        ext_ref[8 : 8 + rows, 128 + cols :] = jnp.transpose(
            jnp.concatenate([e[at, :], pad], axis=0)
        )
        ext_ref[0:8, 0:128] = nw[at, :]
        ext_ref[0:8, 128 + cols :] = ne[at, :]
        ext_ref[8 + rows :, 0:128] = sw[at, :]
        ext_ref[8 + rows :, 128 + cols :] = se[at, :]

    edges = (edge_n, edge_s, edge_w, edge_e)
    halos = (halo_n, halo_s, halo_w, halo_e, halo_nw, halo_ne, halo_sw, halo_se)
    redges = (redge_n, redge_s, redge_w, redge_e)
    rhalos = (rhalo_n, rhalo_s, rhalo_w, rhalo_e, rhalo_nw, rhalo_ne, rhalo_sw, rhalo_se)

    planes[...] = jnp.concatenate(split(pkg_x[own, :]), axis=1)
    ids.wait()
    wanted = jnp.concatenate([ids_got[j] for j in range(nd)], axis=0)
    near = wanted - (lax.broadcasted_iota(jnp.int32, wanted.shape, 1) + me * blocks)
    for q in range(blocks // 256):
        for p in range(2):
            hot[q, :, 128 * p : 128 * p + 128] = jnp.where(
                near == 256 * q + 128 * p, 1.0, 0.0
            ).astype(BF16)

    def pick_rows(source, offset, into):
        both = jnp.zeros((nblk, 256), F32)
        for q in range(blocks // 256):
            both += jnp.dot(
                hot[q], source[offset + q * 256 : offset + q * 256 + 256, :],
                preferred_element_type=F32,
            )
        into[...] = both[:, :128] + both[:, 128:]

    pick_rows(planes, 0, start_ref)
    for j in range(nd):
        rows_out[j] = start_ref[j * cap : (j + 1) * cap, :]
    rows_x = Exchange(nd, me, rows_out, rows_got, sem_rows)
    rows_x.start()
    rows_x.keep()

    lane = lax.broadcasted_iota(jnp.int32, (nblk, 128), 1)
    sub = lax.broadcasted_iota(jnp.int32, (nblk, 128), 0)
    mine = jnp.logical_or(lane == sub, lane == sub + 64)
    in_lanes = jnp.sum(jnp.where(mine, wanted.astype(F32), 0.0), axis=0, keepdims=True)
    id_rows = pl.ds(nblk, 8)
    items[mg, nblk:, :] = jnp.broadcast_to(in_lanes, (8, 128))
    ids_part = remote(
        items.at[mg, id_rows], items.at[mg, id_rows], sem_ids_part.at[0], sem_ids_part.at[1],
        grp=part,
    )
    ids_part.start()

    loads[5].wait()
    inverse = 1.0 / (4.0 + shunt_ref[...] + acc[0])
    set_edges(0, vx, volt_ref[...], *edges)
    set_edges(1, dx, inverse, *edges)
    early = halo_copies(*edges, *halos, sem_halo)
    for copy in early:
        copy.start()

    def build(t, carry):
        at = pl.ds(pl.multiple_of(t * 128, 128), 128)
        ids_at = pat_x[:, at] + (128 + 64 - me * blocks - t * 128)
        weights = wt_x[:, at]
        source = lax.broadcasted_iota(jnp.int32, (256, 128), 0)
        matrix = jnp.zeros((256, 128), F32)
        for k in range(ids_at.shape[0]):
            matrix += jnp.where(source == ids_at[k : k + 1, :], weights[k : k + 1, :], 0.0)
        wmat[t] = jnp.concatenate(split(jnp.transpose(matrix)), axis=0)
        return carry

    lax.fori_loop(1, tiles - 1, build, 0)

    rows_x.wait()
    for j in range(nd):
        start_ref[j * cap : (j + 1) * cap, :] = rows_got[j]
    scatter(
        lambda at: jnp.where(node_ref[at, :] >= 0, cond_ref[at, :] * start_ref[at, :], 0.0), 1
    )
    loads[6].wait()
    set_edges(0, rx, acc[1] - load_ref[...], *redges)
    late = halo_copies(*redges, *rhalos, sem_rhalo)
    for copy in late:
        copy.start()
    for copy in early:
        copy.wait_recv()
    set_halos(0, vx, *halos)
    set_halos(1, dx, *halos)
    height, width = rows + 16, cols + 256
    grow = lax.broadcasted_iota(jnp.int32, (height, width), 0) + (mg * rows - 8)
    gcol = lax.broadcasted_iota(jnp.int32, (height, width), 1) + (me * cols - 128)
    inside = (grow >= 0) & (grow < ng * rows) & (gcol >= 0) & (gcol < nd * cols)
    v = jnp.where(inside, vx[...], 0.0)
    for copy in late:
        copy.wait_recv()
    set_halos(0, rx, *rhalos)
    r = rx[...]
    inv = dx[...]
    for weight in sweep_weights(SWEEPS):
        beside = (
            pltpu.roll(v, 1, 0)
            + pltpu.roll(v, height - 1, 0)
            + pltpu.roll(v, 1, 1)
            + pltpu.roll(v, width - 1, 1)
        )
        v = jnp.where(inside, v + weight * ((r + beside) * inv - v), 0.0)
    final = v[middle]
    die_v[...] = final
    halves = jnp.concatenate(split(final), axis=0)

    def currents(it, carry):
        at = pl.ds(pl.multiple_of(it * chunk, chunk), chunk)
        node = node_ref[at, :]
        row = jnp.right_shift(node, shift)
        rhs = jnp.concatenate([onecol[it * chunk + i] for i in range(chunk)], axis=1)
        both = jnp.dot(halves, rhs, preferred_element_type=F32)
        by_row = both[:rows] + both[rows:]
        seen = [
            jnp.sum(
                jnp.where(row_iota == row[i : i + 1, :], by_row[:, 128 * i : 128 * i + 128], 0.0),
                axis=0,
                keepdims=True,
            )
            for i in range(chunk)
        ]
        flow = jnp.where(
            node >= 0, cond_ref[at, :] * (start_ref[at, :] - jnp.concatenate(seen, axis=0)), 0.0
        )
        for i in range(chunk // cap):
            cur_out[it * (chunk // cap) + i] = flow[i * cap : (i + 1) * cap]
        return carry


    def two_currents(it, carry):
        currents(2 * it, carry)
        return currents(2 * it + 1, carry)

    lax.fori_loop(0, steps // 2, two_currents, 0)
    cur_x = Exchange(nd, me, cur_out, cur_got, sem_cur)
    cur_p = Exchange(nd, me, cur_out, cur_part, sem_cur_part, grp=part)
    cur_x.start()
    cur_p.start()
    cur_x.keep()

    for copy in consts:
        copy.wait_recv()
    lax.fori_loop(0, 2, lambda i, carry: build(i * (tiles - 1), carry), 0)
    rdiag[...] = 1.0 / diag_x[...]
    for q in range(ITERS + 1):
        x_s[q, 0:64, :] = jnp.zeros((64, 256), BF16)
        x_s[q, 64 + ext :, :] = jnp.zeros((64, 256), BF16)
    x_s[0, 64 : 64 + ext, :] = jnp.concatenate(split(pkg_x[...]), axis=1)
    inf_x[0:32, :] = jnp.zeros((32, 128), F32)
    inf_x[ext - 32 :, :] = jnp.zeros((32, 128), F32)
    total[...] = jnp.zeros((blocks, 256), F32)
    loads[7].wait()

    sent = []
    core_of = {}

    def ahead(direction, hops, cc):
        return index(h, lax.rem(y + (hops if direction == 0 else ny - hops), ny), cc)

    def pass_on(slot, direction, dist, k, hops=1):
        copy = remote(
            items.at[slot], items.at[slot],
            sem_ring.at[0, direction, dist, k], sem_ring.at[1, direction, dist, k],
            grp=ahead(direction, hops, c),
        )
        copy.start()
        sent.append(copy)

    def to_core(slot, key):
        n = len(core_of)
        copy = remote(
            items.at[slot], items.at[slot], sem_core.at[0, n], sem_core.at[1, n], grp=core
        )
        copy.start()
        core_of[key] = copy

    def held(direction, dist, k, cc):
        yy = lax.rem(y + ny - dist, ny) if direction == 0 else lax.rem(y + dist, ny)
        return index(h if k == 0 else 1 - h, yy, cc)

    reach = {(0, 0): half, (0, 1): half - 1, (1, 0): half - 1, (1, 1): half}
    first_lanes = lax.broadcasted_iota(jnp.int32, (1, 128), 1) < 64

    def add_group(slots):
        def ids_of(slot):
            return items[slot, nblk : nblk + 1, :]

        pair_ids = [
            jnp.where(first_lanes, ids_of(slots[2 * p]), ids_of(slots[2 * p + 1])).astype(
                jnp.int32
            )
            - me * blocks
            for p in range(2)
        ]
        flows = []
        for slot in slots:
            flows.append(items[slot, :nblk, :])
            if nblk < 64:
                flows.append(jnp.zeros((64 - nblk, 128), F32))
        rhs = jnp.concatenate(split(jnp.concatenate(flows, axis=0)), axis=1)
        target = lax.broadcasted_iota(jnp.int32, (blocks, 128), 0)
        lhs = jnp.concatenate(
            [jnp.where(target == i, 1.0, 0.0).astype(BF16) for i in pair_ids], axis=1
        )
        total[...] += jnp.dot(lhs, rhs, preferred_element_type=F32)

    def keys_of(dist):
        keys = [
            (direction, dist, k)
            for k in range(2)
            for direction in range(2)
            if reach[direction, k] >= dist
        ]
        return keys + (["own", "part"] if dist == half else [])

    def group(dist, cc):
        slots = []
        for key in keys_of(dist):
            if key == "own":
                slots.append(index(h, y, cc))
            elif key == "part":
                slots.append(index(1 - h, y, cc))
            else:
                slots.append(held(*key, cc))
        return slots

    def core_group(dist):
        for key in keys_of(dist):
            core_of[key].wait_recv()
        add_group(group(dist, 1 - c))

    cur_x.wait()
    for j in range(nd):
        items[mg, j * cap : (j + 1) * cap, :] = cur_got[j]
    for direction in range(2):
        if reach[direction, 0] >= 2:
            pass_on(mg, direction, 2, 0, 2)
    for direction in range(2):
        if reach[direction, 0] >= 1:
            pass_on(mg, direction, 1, 0)
    to_core(mg, "own")
    ids_part.wait_recv()
    cur_p.wait()
    for j in range(nd):
        items[part, j * cap : (j + 1) * cap, :] = cur_part[j]
    for direction in range(2):
        if reach[direction, 1] >= 2:
            pass_on(part, direction, 2, 1, 2)
    for direction in range(2):
        if reach[direction, 1] >= 1:
            pass_on(part, direction, 1, 1)
    to_core(part, "part")
    order = [2, 1, *range(3, half + 1)] if half > 1 else [1]
    for step, dist in enumerate(order):
        for k in range(2):
            for direction in range(2):
                if reach[direction, k] >= dist:
                    slot = held(direction, dist, k, c)
                    remote(
                        items.at[slot], items.at[slot],
                        sem_ring.at[0, direction, dist, k], sem_ring.at[1, direction, dist, k],
                        grp=right if direction == 0 else left,
                    ).wait_recv()
                    if dist == 2:
                        for hops in (2, 1):
                            if reach[direction, k] >= dist + hops:
                                pass_on(slot, direction, dist + hops, k, hops)
                    to_core(slot, (direction, dist, k))
        add_group(group(dist, c))
        if step > 0:
            core_group(order[step - 1])
    core_group(order[-1])

    inf_x[own, :] = total[:, :128] + total[:, 128:]
    infs = [
        remote(
            inf_x.at[pl.ds(src, 96)], inf_x.at[pl.ds(dst, 96)],
            sem_inf.at[0, k], sem_inf.at[1, k], die=to,
        )
        for k, (src, dst, to) in enumerate(
            ((128, 128 + blocks, west), (32 + blocks, 32, east))
        )
    ]
    for copy in infs:
        copy.start()
    coup = jnp.concatenate(split(coup_ref[...]), axis=1)

    def tile(iteration, t):
        start = t * 128
        at = pl.ds(start, 128)
        near = jnp.dot(
            wmat[t], x_s[iteration - 1, pl.ds(start, 256), :], preferred_element_type=F32
        )
        here = x_s[iteration - 1, pl.ds(start + 64, 128), :]
        both = jnp.concatenate([here[:, :128], here[:, 128:]], axis=0)
        coupled = near + jnp.dot(both, coup, preferred_element_type=F32)
        coupled = coupled[:128] + coupled[128:]
        coupled = coupled[:, :128] + coupled[:, 128:]
        value = (-inf_x[at, :] - coupled) * rdiag[at, :]
        if iteration == ITERS:
            plane_v[start - 128 : start, :] = value
        x_s[iteration, pl.ds(start + 64, 128), :] = jnp.concatenate(split(value), axis=1)

    def pairs(iteration, begin, end):
        for i in range(begin, end):
            tile(iteration, i)
            tile(iteration, tiles - 1 - i)

    deep = tiles // 2
    for iteration in range(1, ITERS + 1):
        pairs(iteration, min(iteration, deep), deep)
    for copy in infs:
        copy.wait_recv()
    for iteration in range(1, ITERS + 1):
        pairs(iteration, 1 if iteration == ITERS else 0, min(iteration, deep))

    rows_x.drain()
    pick_rows(x_s.at[ITERS], 64 + 128, start_ref)
    for j in range(nd):
        rows_out[j] = start_ref[j * cap : (j + 1) * cap, :]
    bump_x = Exchange(nd, me, rows_out, rows_got, sem_bump)
    bump_x.start()
    bump_x.keep()
    for x in (ids, cur_x, cur_p):
        x.drain()
    for copy in sent + list(core_of.values()) + [ids_part] + consts + infs + early + late:
        copy.wait_send()
    bump_x.wait()
    for j in range(nd):
        bump_v[j * cap : (j + 1) * cap, :] = rows_got[j]
    bump_x.drain()


def local(
    nd, ng,
    die_volt, die_load, die_shunt, bump_node, bump_block, bump_cond,
    pkg_volt, pkg_diag, pkg_pattern, pkg_weight, block_coupling,
):
    nblk = bump_node.shape[0]
    cap = nblk // nd
    blocks = pkg_volt.shape[0]
    rows, cols = die_volt.shape
    ext = blocks + 256
    knb = pkg_pattern.shape[0]
    anywhere = pl.BlockSpec(memory_space=pl.ANY)
    dma = pltpu.SemaphoreType.DMA

    def buf(*shape, dtype=F32):
        return pltpu.VMEM(shape, dtype)

    def strip_set(depth):
        return [
            buf(2, depth, 128), buf(2, depth, 128), buf(depth, 128), buf(depth, 128),
            buf(2, depth, 128), buf(2, depth, 128), buf(depth, 128), buf(depth, 128),
            buf(depth, 128), buf(depth, 128), buf(depth, 128), buf(depth, 128),
        ]

    results = pl.pallas_call(
        functools.partial(kernel, nd, ng, cap, blocks),
        out_shape=(
            pltpu.VMEM((rows, cols), F32),
            pltpu.VMEM((blocks, 128), F32),
            pltpu.VMEM((nblk, 128), F32),
        ),
        in_specs=[anywhere] * 11,
        out_specs=(pl.BlockSpec(memory_space=pltpu.VMEM),) * 3,
        scratch_shapes=[
            pltpu.SMEM((nblk,), jnp.int32), buf(nblk, 128, dtype=jnp.int32), buf(nblk, 128),
            buf(rows, cols), buf(rows, cols), buf(rows, cols), buf(128, 128),
            buf(nd, cap, 128, dtype=jnp.int32), buf(nd, cap, 128, dtype=jnp.int32),
            buf(nd, cap, 128), buf(nd, cap, 128),
            buf(nd, cap, 128), buf(nd, cap, 128), buf(nd, cap, 128),
            buf(nblk, 128),
            buf(blocks // 256, nblk, 256, dtype=BF16),
            buf(blocks, 256, dtype=BF16),
            buf(nblk, cols, 128, dtype=BF16),
            buf(2, rows, cols),
            buf(rows + 16, cols + 256), buf(rows + 16, cols + 256), buf(rows + 16, cols + 256),
            *strip_set(16),
            *strip_set(8),
            buf(ng, nblk + 8, 128),
            buf(ITERS + 1, ext + 128, 256, dtype=BF16),
            buf(ext, 128),
            buf(ext, 128), buf(ext, 128), buf(ext, 128),
            buf(knb, ext, dtype=jnp.int32), buf(knb, ext),
            buf(ext // 128, 256, 256, dtype=BF16),
            buf(blocks, 256),
            dma((11,)), dma((2, nd)), dma((2, nd)), dma((2, nd)), dma((2, nd)),
            dma((2, 8)), dma((2, 8)), dma((2, 8)), dma((2,)),
            dma((2, 2, ng // 8 + 2, 2)), dma((2, ng // 2)), dma((2, 2)), dma((2, nd)),
        ],
        compiler_params=pltpu.CompilerParams(collective_id=0, has_side_effects=True),
        name="coupling_round",
    )(
        bump_block, bump_node, bump_cond, die_volt, die_load, die_shunt,
        pkg_volt, pkg_diag, pkg_pattern, pkg_weight, block_coupling,
    )
    return pl.pallas_call(
        hand_over,
        out_shape=tuple(jax.ShapeDtypeStruct(r.shape, F32) for r in results),
        in_specs=[pl.BlockSpec(memory_space=pltpu.VMEM)] * 3,
        out_specs=(anywhere,) * 3,
        scratch_shapes=[dma((16,))],
        name="hand_over",
    )(*[pltpu.with_memory_space_constraint(r, pltpu.VMEM) for r in results])


def hand_over(*refs):
    sources, targets, sem = refs[:3], refs[3:6], refs[6]
    copies = []
    for k, (src, dst) in enumerate(zip(sources, targets)):
        count = 8 if k == 1 else 2
        depth = src.shape[0] // count
        for p in range(count):
            at = pl.ds(p * depth, depth)
            copies.append(pltpu.make_async_copy(src.at[at], dst.at[at], sem.at[len(copies)]))
    for copy in copies:
        copy.start()
    for copy in copies:
        copy.wait()


def solution(mesh):
    return jax.shard_map(
        functools.partial(local, mesh.shape["die"], mesh.shape["grp"]),
        mesh=mesh,
        in_specs=(
            P("grp", "die"),
            P("grp", "die"),
            P("grp", "die"),
            P(("grp", "die"), None),
            P(("grp", "die")),
            P(("grp", "die"), None),
            P("die", None),
            P("die", None),
            P(None, "die"),
            P(None, "die"),
            P(),
        ),
        out_specs=(P("grp", "die"), P("die", None), P(("grp", "die"), None)),
        check_vma=False,
    )
```
